32 devices in a mesh: dp: 8 (over z, x), tensor: 4 (over y, core).
Axes of the slice: x: 2, y: 2, z: 4, core: 2. Of those that a mesh axis runs over, the one named last changes fastest.
Arguments:
- tokens: bfloat16 [4096, 1024], P(('dp', 'tensor')), may hold values from -6 to 6
- cotangent: bfloat16 [4096, 1024], P(('dp', 'tensor')), may hold values from -6 to 6
- norm1_gain: bfloat16 [1024], P('dp'), may hold values from 0.5 to 1.5
- w_query: bfloat16 [1024, 1024], P('dp', 'tensor'), may hold values from -0.1875 to 0.1875
- w_key: bfloat16 [1024, 1024], P('dp', 'tensor'), may hold values from -0.1875 to 0.1875
- w_value: bfloat16 [1024, 2048], P('dp', 'tensor'), may hold values from -0.1875 to 0.1875
- w_gate_out: bfloat16 [1024, 2048], P('dp', 'tensor'), may hold values from -0.1875 to 0.1875
- w_out: bfloat16 [1024, 2048], P('dp', 'tensor'), may hold values from -0.1875 to 0.1875
- w_beta: bfloat16 [1024, 8], P('dp', 'tensor'), may hold values from -0.1875 to 0.1875
- w_alpha: bfloat16 [1024, 8], P('dp', 'tensor'), may hold values from -0.1875 to 0.1875
- conv_query: bfloat16 [128, 8, 4], P('dp', 'tensor'), may hold values from -3 to 3
- conv_key: bfloat16 [128, 8, 4], P('dp', 'tensor'), may hold values from -3 to 3
- conv_value: bfloat16 [256, 8, 4], P('dp', 'tensor'), may hold values from -3 to 3
- a_log: bfloat16 [8], P('tensor'), may hold values from 0 to 2.765625
- dt_bias: bfloat16 [8], P('tensor'), may hold values from -6.875 to -2.296875
- head_gain: bfloat16 [256, 8], P('dp', 'tensor'), may hold values from 0.5 to 1.5
- norm2_gain: bfloat16 [1024], P('dp'), may hold values from 0.5 to 1.5
- w_up_gate: bfloat16 [1024, 2816], P('dp', 'tensor'), may hold values from -0.1875 to 0.1875
- w_up: bfloat16 [1024, 2816], P('dp', 'tensor'), may hold values from -0.1875 to 0.1875
- w_down: bfloat16 [1024, 2816], P('dp', 'tensor'), may hold values from -0.109375 to 0.109375
Outputs:
- out: bfloat16 [4096, 1024], P(('dp', 'tensor'))
- grad_tokens: float32 [4096, 1024], P(('dp', 'tensor'))
- grad_norm1_gain: float32 [1024], P('dp')
- grad_w_query: float32 [1024, 1024], P('dp', 'tensor')
- grad_w_key: float32 [1024, 1024], P('dp', 'tensor')
- grad_w_value: float32 [1024, 2048], P('dp', 'tensor')
- grad_w_gate_out: float32 [1024, 2048], P('dp', 'tensor')
- grad_w_out: float32 [1024, 2048], P('dp', 'tensor')
- grad_w_beta: float32 [1024, 8], P('dp', 'tensor')
- grad_w_alpha: float32 [1024, 8], P('dp', 'tensor')
- grad_conv_query: float32 [128, 8, 4], P('dp', 'tensor')
- grad_conv_key: float32 [128, 8, 4], P('dp', 'tensor')
- grad_conv_value: float32 [256, 8, 4], P('dp', 'tensor')
- grad_a_log: float32 [8], P('tensor')
- grad_dt_bias: float32 [8], P('tensor')
- grad_head_gain: float32 [256, 8], P('dp', 'tensor')
- grad_norm2_gain: float32 [1024], P('dp')
- grad_w_up_gate: float32 [1024, 2816], P('dp', 'tensor')
- grad_w_up: float32 [1024, 2816], P('dp', 'tensor')
- grad_w_down: float32 [1024, 2816], P('dp', 'tensor')
The draws below stay inside these ranges and needn't reach their ends.
All inputs are finite; a program needn't handle non-finite values.
Results may differ from the reference program's by a relative error of at most 0.012.
Values may be sent and summed in bfloat16 or wider, within the bound.
A program may use at most 128 MiB of HBM per device.

```python
from functools import partial
import jax
import jax.numpy as jnp
from jax import lax

D = 1024
H = 8
DK = 128
DV = 256
FF = 2816
CONV = 4
BLOCK = 64
SEQ = 512
TOKENS = 4096


def level_of(own_key, dims, cuts, smallest, high):
    factor_of = 1.0
    for dim, parts in cuts:
        draws = jax.random.uniform(jax.random.fold_in(jax.random.fold_in(own_key, 6), dim), (parts,), jnp.float32, smallest / len(cuts), high / len(cuts))
        factor_of = factor_of * jnp.repeat(jnp.exp(draws), dims[dim] // parts).reshape((-1,) + (1,) * (len(dims) - 1 - dim))
    return factor_of


def centred(key, extent, width, most, cuts=(), kind=jnp.bfloat16):
    factor_of = level_of(key, extent, cuts, -0.22, 0.18) if cuts else 1.0
    drawn = jax.random.normal(key, extent, jnp.float32) * width * factor_of
    return jnp.minimum(jnp.maximum(drawn, -most), most).astype(kind)


def setup_inputs(seed: int = 0) -> dict:
    splits = jax.random.split(jax.random.key(seed), 21)
    tokens = centred(splits[0], (TOKENS, D), 1.0, 6.0, ((0, 32),))
    cotangent = centred(splits[1], (TOKENS, D), 1.0, 6.0, ((0, 32),))
    norm1_gain = jnp.clip(1.0 + 0.1 * jax.random.normal(splits[2], (D,), jnp.float32), 0.5, 1.5).astype(jnp.bfloat16)
    w_query = centred(splits[3], (D, H * DK), D ** -0.5, 0.1875, ((0, 8), (1, 4)))
    w_key = centred(splits[4], (D, H * DK), D ** -0.5, 0.1875, ((0, 8), (1, 4)))
    w_value = centred(splits[5], (D, H * DV), D ** -0.5, 0.1875, ((0, 8), (1, 4)))
    w_gate_out = centred(splits[6], (D, H * DV), D ** -0.5, 0.1875, ((0, 8), (1, 4)))
    w_out = centred(splits[7], (D, H * DV), (H * DV // 2) ** -0.5, 0.1875, ((0, 8), (1, 4)))
    w_beta = centred(splits[8], (D, H), D ** -0.5, 0.1875, ((0, 8), (1, 4)))
    w_alpha = centred(splits[9], (D, H), D ** -0.5, 0.1875, ((0, 8), (1, 4)))
    conv_query = centred(splits[10], (DK, H, CONV), CONV ** -0.5, 3.0, ((0, 8), (1, 4)))
    conv_key = centred(splits[11], (DK, H, CONV), CONV ** -0.5, 3.0, ((0, 8), (1, 4)))
    conv_value = centred(splits[12], (DV, H, CONV), CONV ** -0.5, 3.0, ((0, 8), (1, 4)))
    a_log = jnp.clip(2.765625 * jax.random.uniform(splits[13], (H,), jnp.float32) ** level_of(splits[13], (H,), ((0, 4),), -0.2, 0.2), 0.0, 2.765625).astype(jnp.bfloat16)
    dt_bias = jnp.clip(-6.875 + 4.578125 * jax.random.uniform(splits[14], (H,), jnp.float32) ** level_of(splits[14], (H,), ((0, 4),), -0.2, 0.2), -6.875, -2.296875).astype(jnp.bfloat16)
    head_gain = jnp.clip(1.0 + 0.1 * jax.random.normal(splits[15], (DV, H), jnp.float32), 0.5, 1.5).astype(jnp.bfloat16)
    norm2_gain = jnp.clip(1.0 + 0.1 * jax.random.normal(splits[16], (D,), jnp.float32), 0.5, 1.5).astype(jnp.bfloat16)
    w_up_gate = centred(splits[17], (D, FF), D ** -0.5, 0.1875, ((0, 8), (1, 4)))
    w_up = centred(splits[18], (D, FF), D ** -0.5, 0.1875, ((0, 8), (1, 4)))
    w_down = centred(splits[19], (D, FF), FF ** -0.5, 0.109375, ((0, 8), (1, 4)))
    return {"tokens": tokens, "cotangent": cotangent, "norm1_gain": norm1_gain, "w_query": w_query, "w_key": w_key, "w_value": w_value, "w_gate_out": w_gate_out, "w_out": w_out, "w_beta": w_beta, "w_alpha": w_alpha, "conv_query": conv_query, "conv_key": conv_key, "conv_value": conv_value, "a_log": a_log, "dt_bias": dt_bias, "head_gain": head_gain, "norm2_gain": norm2_gain, "w_up_gate": w_up_gate, "w_up": w_up, "w_down": w_down}


epsilon = 1e-06
highest = lax.Precision.HIGHEST
contract_rows = (((0,), (0,)), ((), ()))
contract_cols = (((1,), (1,)), ((), ()))

def norm_forward(row_values):
    row_scale = lax.rsqrt(lax.optimization_barrier(jnp.mean(row_values * row_values, axis=-1, keepdims=True)) + epsilon)
    return (row_scale, row_values * row_scale)

def norm_backward(grad_normed, unit_values, row_scale, gain_values):
    grad_unit = grad_normed * gain_values
    return row_scale * (grad_unit - unit_values * lax.optimization_barrier(jnp.mean(grad_unit * unit_values, axis=-1, keepdims=True)))

def short_conv(inputs, weights):
    tap_count = weights.shape[1]
    row_count = inputs.shape[0]
    padded = jnp.pad(inputs, ((tap_count - 1, 0), (0, 0)))
    result = jnp.zeros_like(inputs)
    for offset in range(tap_count):
        result = result + padded[offset:offset + row_count] * weights[:, offset]
    return result

def unit_length(values):
    return values * lax.rsqrt(lax.optimization_barrier(jnp.sum(values * values, axis=-1, keepdims=True)) + epsilon)

def split_heads(matrix_in, head_count):
    row_count, total_width = matrix_in.shape
    return jnp.swapaxes(matrix_in.reshape(row_count, head_count, total_width // head_count), 0, 1)

def channel_weights(conv_weights):
    key_dim, head_count, tap_count = conv_weights.shape
    return jnp.swapaxes(conv_weights, 0, 1).reshape(head_count * key_dim, tap_count)

def delta_rule(queries, keys_in, values, beta_rows, log_gates):
    head_count, seq_rows, key_dim = queries.shape
    value_dim = values.shape[2]
    block_count = seq_rows // BLOCK

    def blocked(matrix_in):
        return jnp.swapaxes(matrix_in.reshape((head_count, block_count, BLOCK) + matrix_in.shape[2:]), 0, 1)
    lower_incl = jnp.tril(jnp.ones((BLOCK, BLOCK), dtype=bool))
    lower_strict = jnp.tril(jnp.ones((BLOCK, BLOCK), dtype=bool), -1)
    identity_mat = jnp.eye(BLOCK, dtype=jnp.float32)
    solver = jax.vmap(partial(jax.scipy.linalg.solve_triangular, lower=True, unit_diagonal=True))

    def advance(carry_state, pieces):
        query_blk, key_blk, value_blk, beta_blk, gate_blk = pieces
        cum_decay = jnp.cumsum(gate_blk, axis=-1)
        differ = cum_decay[:, :, None] - cum_decay[:, None, :]
        decay_mat = jnp.where(lower_incl, jnp.exp(jnp.where(lower_incl, differ, 0.0)), 0.0)
        key_gram = jnp.einsum('hid,hjd->hij', key_blk, key_blk, precision=highest)
        system = identity_mat + jnp.where(lower_strict, key_gram * decay_mat * beta_blk[:, :, None], 0.0)
        right_side = jnp.concatenate([key_blk * (beta_blk * jnp.exp(cum_decay))[:, :, None], value_blk * beta_blk[:, :, None]], axis=-1)
        solved = solver(system, right_side)
        key_part = solved[..., :key_dim]
        value_part = solved[..., key_dim:]
        fresh_values = value_part - jnp.einsum('hcd,hde->hce', key_part, carry_state, precision=highest)
        scores = jnp.einsum('hid,hjd->hij', query_blk, key_blk, precision=highest) * decay_mat
        output_blk = jnp.einsum('hcd,hde->hce', query_blk * jnp.exp(cum_decay)[:, :, None], carry_state, precision=highest)
        output_blk = output_blk + jnp.einsum('hij,hje->hie', scores, fresh_values, precision=highest)
        final_decay = cum_decay[:, -1]
        carried = jnp.exp(final_decay)[:, None, None] * carry_state
        carry_state = carried + jnp.einsum('hcd,hce->hde', key_blk * jnp.exp(final_decay[:, None] - cum_decay)[:, :, None], fresh_values, precision=highest)
        return (carry_state, output_blk)
    initial = jnp.zeros((head_count, key_dim, value_dim), jnp.float32)
    unused, outputs = lax.scan(advance, initial, (blocked(queries), blocked(keys_in), blocked(values), blocked(beta_rows), blocked(log_gates)))
    return jnp.swapaxes(outputs, 0, 1).reshape(head_count, seq_rows, value_dim)

def mixer_piece(proj_query, proj_key, proj_value, proj_gate, proj_beta, proj_alpha, conv_q_w, conv_k_w, conv_v_w, gain_heads, log_rate, rate_bias):
    head_count = proj_beta.shape[1]
    queries = split_heads(jax.nn.silu(short_conv(proj_query, channel_weights(conv_q_w))), head_count)
    queries = unit_length(queries) * queries.shape[2] ** (-0.5)
    keys_in = unit_length(split_heads(jax.nn.silu(short_conv(proj_key, channel_weights(conv_k_w))), head_count))
    values = split_heads(jax.nn.silu(short_conv(proj_value, channel_weights(conv_v_w))), head_count)
    beta_rows = jax.nn.sigmoid(proj_beta).T
    log_gates = -jnp.exp(log_rate)[:, None] * jax.nn.softplus(proj_alpha + rate_bias).T
    mixed = delta_rule(queries, keys_in, values, beta_rows, log_gates)
    scaled = mixed * lax.rsqrt(lax.optimization_barrier(jnp.mean(mixed * mixed, axis=-1, keepdims=True)) + epsilon) * gain_heads.T[:, None, :]
    gated = scaled * split_heads(jax.nn.silu(proj_gate), head_count)
    return jnp.swapaxes(gated, 0, 1).reshape(gated.shape[1], -1)

def weight_grad(left_in, right_in):
    return lax.dot_general(left_in.astype(jnp.float32), right_in.astype(jnp.float32), contract_rows, preferred_element_type=jnp.float32)

def times_transpose(left_in, right_in):
    return lax.dot_general(left_in.astype(jnp.float32), right_in.astype(jnp.float32), contract_cols, preferred_element_type=jnp.float32)

def reference(tokens, cotangent, norm1_gain, w_query, w_key, w_value, w_gate_out, w_out, w_beta, w_alpha, conv_query, conv_key, conv_value, a_log, dt_bias, head_gain, norm2_gain, w_up_gate, w_up, w_down):
    small_params = tuple((param.astype(jnp.float32) for param in (conv_query, conv_key, conv_value, head_gain, a_log, dt_bias)))
    gain_one = norm1_gain.astype(jnp.float32)
    gain_two = norm2_gain.astype(jnp.float32)
    mixer_mats = (w_query, w_key, w_value, w_gate_out, w_beta, w_alpha)
    grad_params = (norm1_gain, w_query, w_key, w_value, w_gate_out, w_out, w_beta, w_alpha, conv_query, conv_key, conv_value, a_log, dt_bias, head_gain, norm2_gain, w_up_gate, w_up, w_down)

    def one_sequence(totals, paired):
        seq_tokens, seq_cot = paired
        row_values = seq_tokens.astype(jnp.float32)
        scale_one, unit_one = norm_forward(row_values)
        normed_one = (unit_one * gain_one).astype(jnp.bfloat16)
        projected = [jnp.dot(normed_one.astype(jnp.float32), weight.astype(jnp.float32), preferred_element_type=jnp.float32) for weight in mixer_mats]
        mixed_full, pullback = jax.vjp(mixer_piece, *projected, *small_params)
        mixed = mixed_full.astype(jnp.bfloat16)
        middle = row_values + times_transpose(mixed, w_out)
        scale_two, unit_two = norm_forward(middle)
        normed_two = (unit_two * gain_two).astype(jnp.bfloat16)
        up_gate = jnp.dot(normed_two.astype(jnp.float32), w_up_gate.astype(jnp.float32), preferred_element_type=jnp.float32)
        up_lin = jnp.dot(normed_two.astype(jnp.float32), w_up.astype(jnp.float32), preferred_element_type=jnp.float32)
        hidden = (jax.nn.silu(up_gate) * up_lin).astype(jnp.bfloat16)
        result = (middle + times_transpose(hidden, w_down)).astype(jnp.bfloat16)
        grad_hidden = jnp.dot(seq_cot.astype(jnp.float32), w_down.astype(jnp.float32), preferred_element_type=jnp.float32)
        grad_down = weight_grad(seq_cot, hidden)
        gate_sigmoid = jax.nn.sigmoid(up_gate)
        grad_gate = (grad_hidden * up_lin * gate_sigmoid * (1.0 + up_gate * (1.0 - gate_sigmoid))).astype(jnp.bfloat16)
        grad_lin = (grad_hidden * up_gate * gate_sigmoid).astype(jnp.bfloat16)
        grad_up_gate = weight_grad(normed_two, grad_gate)
        grad_up = weight_grad(normed_two, grad_lin)
        grad_normed_two = times_transpose(grad_gate, w_up_gate) + times_transpose(grad_lin, w_up)
        grad_gain_two = lax.optimization_barrier(jnp.sum(grad_normed_two * unit_two, axis=0))
        grad_middle = seq_cot.astype(jnp.float32) + norm_backward(grad_normed_two, unit_two, scale_two, gain_two)
        grad_mid = grad_middle.astype(jnp.bfloat16)
        grad_out_w = weight_grad(grad_mid, mixed)
        grad_mixed = jnp.dot(grad_mid.astype(jnp.float32), w_out.astype(jnp.float32), preferred_element_type=jnp.float32)
        pulled = pullback(grad_mixed)
        grad_proj = [grad_piece.astype(jnp.bfloat16) for grad_piece in pulled[:6]]
        grad_mats = [weight_grad(normed_one, grad_piece) for grad_piece in grad_proj]
        grad_normed_one = sum((times_transpose(grad_piece, weight) for grad_piece, weight in zip(grad_proj, mixer_mats)))
        grad_gain_one = lax.optimization_barrier(jnp.sum(grad_normed_one * unit_one, axis=0))
        grad_rows = grad_middle + norm_backward(grad_normed_one, unit_one, scale_one, gain_one)
        grads = (grad_gain_one, grad_mats[0], grad_mats[1], grad_mats[2], grad_mats[3], grad_out_w, grad_mats[4], grad_mats[5], pulled[6], pulled[7], pulled[8], pulled[10], pulled[11], pulled[9], grad_gain_two, grad_up_gate, grad_up, grad_down)
        totals = tuple((total + grad_piece for total, grad_piece in zip(totals, grads)))
        return (totals, (result, grad_rows))
    initial = tuple((jnp.zeros(param.shape, jnp.float32) for param in grad_params))
    seq_tokens_all = tokens.reshape(-1, SEQ, D)
    seq_cot_all = cotangent.reshape(-1, SEQ, D)
    totals, stacked = lax.scan(one_sequence, initial, (seq_tokens_all, seq_cot_all))
    result_all = stacked[0].reshape(-1, D)
    grad_all = stacked[1].reshape(-1, D)
    return (result_all, grad_all, totals[0], totals[1], totals[2], totals[3], totals[4], totals[5], totals[6], totals[7], totals[8], totals[9], totals[10], totals[11], totals[12], totals[13], totals[14], totals[15], totals[16], totals[17])
```

```python
import jax
import jax.numpy as jnp
from jax import lax
from jax.experimental import pallas as pl
from jax.experimental.pallas import tpu as pltpu
from jax.sharding import PartitionSpec as P

epsilon = 1e-06
CHUNK = 128
LANES = 128
contract_rows = (((0,), (0,)), ((), ()))
contract_cols = (((1,), (1,)), ((), ()))
contract_plain = (((1,), (0,)), ((), ()))
highest = lax.Precision.HIGHEST


def norm_forward(row_values):
    row_scale = lax.rsqrt(jnp.mean(row_values * row_values, axis=-1, keepdims=True) + epsilon)
    return (row_scale, row_values * row_scale)


def norm_backward(grad_normed, unit_values, row_scale, gain_values):
    grad_unit = grad_normed * gain_values
    return row_scale * (
        grad_unit - unit_values * jnp.mean(grad_unit * unit_values, axis=-1, keepdims=True)
    )


def weight_grad(left_in, right_in):
    return lax.dot_general(left_in, right_in, contract_rows, preferred_element_type=jnp.float32)


def times_transpose(left_in, right_in):
    return lax.dot_general(left_in, right_in, contract_cols, preferred_element_type=jnp.float32)


def exact_dot(left_in, right_in, dims=contract_plain):
    return lax.dot_general(
        left_in, right_in, dims, precision=highest, preferred_element_type=jnp.float32
    )


def silu(values):
    return values * lax.logistic(values)


def unit_length(values):
    return values * lax.rsqrt(jnp.sum(values * values, axis=-1, keepdims=True) + epsilon)


def triangle_masks(size):
    row = lax.broadcasted_iota(jnp.int32, (size, size), 0)
    col = lax.broadcasted_iota(jnp.int32, (size, size), 1)
    return row, col


def unit_lower_inverse(lower):
    size = lower.shape[0]
    row, col = triangle_masks(size)
    inverse = jnp.where(row == col, 1.0, 0.0)
    bit = 0
    while (1 << bit) < size:
        joined = ((row >> (bit + 1)) == (col >> (bit + 1))) & ((row >> bit) != (col >> bit))
        part = jnp.where(joined, lower, 0.0)
        if bit == 0:
            inverse = inverse - part
        else:
            inverse = inverse - exact_dot(inverse, exact_dot(part, inverse))
        bit += 1
    return inverse


@jax.custom_vjp
def known_inverse(lower, inverse):
    return inverse


def known_inverse_fwd(lower, inverse):
    return inverse, inverse


def known_inverse_bwd(inverse, grad):
    turned = inverse.T
    return -exact_dot(exact_dot(turned, grad), turned), jnp.zeros_like(inverse)


known_inverse.defvjp(known_inverse_fwd, known_inverse_bwd)


def mixer_chunk(conv_q, conv_k, conv_v, proj_gate, beta, gate, gain, state, inverter):
    size, key_dim = conv_q.shape
    row, col = triangle_masks(size)
    strict = row > col
    lower = row >= col
    query = unit_length(silu(conv_q)) * key_dim ** (-0.5)
    key = unit_length(silu(conv_k))
    value = silu(conv_v)
    wide = jnp.broadcast_to(gate, (size, size))
    decay_col = jnp.sum(jnp.where(lower, wide.T, 0.0), axis=1, keepdims=True)
    decay_row = jnp.sum(jnp.where(row <= col, wide, 0.0), axis=0, keepdims=True)
    decay_end = jnp.sum(gate, axis=0, keepdims=True)
    differ = jnp.where(strict, decay_col - decay_row, 0.0)
    decay = jnp.where(lower, jnp.exp(differ), 0.0)
    system = jnp.where(strict, exact_dot(key, key, contract_cols) * decay * beta, 0.0)
    inverse = inverter(system)
    grown = jnp.exp(decay_col)
    fresh = exact_dot(inverse, value * beta - exact_dot(key * (beta * grown), state))
    scores = exact_dot(query, key, contract_cols) * decay
    mixed = exact_dot(query * grown, state) + exact_dot(scores, fresh)
    new_state = jnp.exp(decay_end) * state + exact_dot(
        key * jnp.exp(decay_end - decay_col), fresh, contract_rows
    )
    scaled = mixed * lax.rsqrt(jnp.mean(mixed * mixed, axis=-1, keepdims=True) + epsilon) * gain
    return scaled * silu(proj_gate), new_state, inverse


def head_slices(head, heads, key_dim, value_dim):
    q_at = head * key_dim
    k_at = (heads + head) * key_dim
    v_at = 2 * heads * key_dim + head * value_dim
    return (
        slice(q_at, q_at + key_dim),
        slice(k_at, k_at + key_dim),
        slice(v_at, v_at + value_dim),
        slice(head * value_dim, (head + 1) * value_dim),
    )


def mixer_forward_kernel(
    heads, key_dim, value_dim, conv_ref, pgate_ref, rates_ref, gain_ref,
    gated_ref, states_ref, inverses_ref, state_ref,
):
    @pl.when(pl.program_id(0) == 0)
    def _():
        state_ref[...] = jnp.zeros_like(state_ref)

    for head in range(heads):
        at_q, at_k, at_v, at_g = head_slices(head, heads, key_dim, value_dim)
        state = state_ref[head]
        gated, new_state, inverse = mixer_chunk(
            conv_ref[:, at_q],
            conv_ref[:, at_k],
            conv_ref[:, at_v],
            pgate_ref[:, at_g],
            rates_ref[:, head : head + 1],
            rates_ref[:, heads + head : heads + head + 1],
            gain_ref[:, at_g],
            state,
            unit_lower_inverse,
        )
        gated_ref[:, at_g] = gated.astype(gated_ref.dtype)
        states_ref[0, head] = state
        inverses_ref[0, head] = inverse
        state_ref[head] = new_state


def mixer_backward_kernel(
    heads, key_dim, value_dim, conv_ref, pgate_ref, rates_ref, gain_ref, states_ref,
    inverses_ref, grad_ref, gconv_ref, gpgate_ref, grates_ref, ggain_ref, gstate_ref,
):
    @pl.when(pl.program_id(0) == 0)
    def _():
        gstate_ref[...] = jnp.zeros_like(gstate_ref)
        ggain_ref[...] = jnp.zeros_like(ggain_ref)

    lane = lax.broadcasted_iota(jnp.int32, grates_ref.shape, 1)
    rates_grad = jnp.zeros(grates_ref.shape, jnp.float32)
    for head in range(heads):
        at_q, at_k, at_v, at_g = head_slices(head, heads, key_dim, value_dim)
        inverse = inverses_ref[0, head]

        def run(*operands):
            gated, new_state, _ = mixer_chunk(
                *operands, lambda system: known_inverse(system, inverse)
            )
            return gated, new_state

        _, pull = jax.vjp(
            run,
            conv_ref[:, at_q],
            conv_ref[:, at_k],
            conv_ref[:, at_v],
            pgate_ref[:, at_g],
            rates_ref[:, head : head + 1],
            rates_ref[:, heads + head : heads + head + 1],
            gain_ref[:, at_g],
            states_ref[0, head],
        )
        pulled = pull((grad_ref[:, at_g], gstate_ref[head]))
        gconv_ref[:, at_q] = pulled[0]
        gconv_ref[:, at_k] = pulled[1]
        gconv_ref[:, at_v] = pulled[2]
        gpgate_ref[:, at_g] = pulled[3]
        rates_grad = jnp.where(lane == head, pulled[4], rates_grad)
        rates_grad = jnp.where(lane == heads + head, pulled[5], rates_grad)
        ggain_ref[:, at_g] += pulled[6]
        gstate_ref[head] = pulled[7]
    grates_ref[...] = rates_grad


def row_block(width, order):
    return pl.BlockSpec((CHUNK, width), lambda step: (order(step), 0))


def mixer_forward(conv_all, proj_gate, rates, gain_row, heads, key_dim, value_dim):
    rows, conv_width = conv_all.shape
    steps = rows // CHUNK
    forward = lambda step: step
    width = heads * value_dim
    return pl.pallas_call(
        lambda *refs: mixer_forward_kernel(heads, key_dim, value_dim, *refs),
        name="mixer_forward",
        grid=(steps,),
        in_specs=[
            row_block(conv_width, forward),
            row_block(width, forward),
            row_block(rates.shape[1], forward),
            pl.BlockSpec((1, width), lambda step: (0, 0)),
        ],
        out_specs=[
            row_block(width, forward),
            pl.BlockSpec((1, heads, key_dim, value_dim), lambda step: (step, 0, 0, 0)),
            pl.BlockSpec((1, heads, CHUNK, CHUNK), lambda step: (step, 0, 0, 0)),
        ],
        out_shape=[
            jax.ShapeDtypeStruct((rows, width), jnp.bfloat16),
            jax.ShapeDtypeStruct((steps, heads, key_dim, value_dim), jnp.float32),
            jax.ShapeDtypeStruct((steps, heads, CHUNK, CHUNK), jnp.float32),
        ],
        scratch_shapes=[pltpu.VMEM((heads, key_dim, value_dim), jnp.float32)],
        cost_estimate=pl.CostEstimate(
            flops=30_000_000_000, bytes_accessed=8_000_000, transcendentals=1_000_000
        ),
    )(conv_all, proj_gate, rates, gain_row)


def mixer_backward(
    conv_all, proj_gate, rates, gain_row, states, inverses, grad_gated, heads, key_dim, value_dim
):
    rows, conv_width = conv_all.shape
    steps = rows // CHUNK
    back = lambda step: steps - 1 - step
    width = heads * value_dim
    return pl.pallas_call(
        lambda *refs: mixer_backward_kernel(heads, key_dim, value_dim, *refs),
        name="mixer_backward",
        grid=(steps,),
        in_specs=[
            row_block(conv_width, back),
            row_block(width, back),
            row_block(rates.shape[1], back),
            pl.BlockSpec((1, width), lambda step: (0, 0)),
            pl.BlockSpec((1, heads, key_dim, value_dim), lambda step: (back(step), 0, 0, 0)),
            pl.BlockSpec((1, heads, CHUNK, CHUNK), lambda step: (back(step), 0, 0, 0)),
            row_block(width, back),
        ],
        out_specs=[
            row_block(conv_width, back),
            row_block(width, back),
            row_block(rates.shape[1], back),
            pl.BlockSpec((1, width), lambda step: (0, 0)),
        ],
        out_shape=[
            jax.ShapeDtypeStruct((rows, conv_width), jnp.float32),
            jax.ShapeDtypeStruct((rows, width), jnp.float32),
            jax.ShapeDtypeStruct(rates.shape, jnp.float32),
            jax.ShapeDtypeStruct((1, width), jnp.float32),
        ],
        scratch_shapes=[pltpu.VMEM((heads, key_dim, value_dim), jnp.float32)],
        cost_estimate=pl.CostEstimate(
            flops=30_000_000_000, bytes_accessed=12_000_000, transcendentals=2_000_000
        ),
    )(conv_all, proj_gate, rates, gain_row, states, inverses, grad_gated)


def exchange_kernel(axis, ranks, scatter, block_ref, got_ref, send_sems, recv_sems):
    me = lax.axis_index(axis)
    barrier = pltpu.get_barrier_semaphore()
    for step in range(1, ranks):
        pl.semaphore_signal(
            barrier,
            inc=1,
            device_id={axis: lax.rem(me + step, ranks)},
            device_id_type=pl.DeviceIdType.MESH,
        )
    pl.semaphore_wait(barrier, ranks - 1)
    copies = []
    for step in range(1, ranks):
        peer = lax.rem(me + step, ranks)
        copy = pltpu.make_async_remote_copy(
            src_ref=block_ref.at[peer] if scatter else block_ref.at[0],
            dst_ref=got_ref.at[me],
            send_sem=send_sems.at[step - 1],
            recv_sem=recv_sems.at[step - 1],
            device_id={axis: peer},
            device_id_type=pl.DeviceIdType.MESH,
        )
        copy.start()
        copies.append(copy)
    got_ref[me] = block_ref[me] if scatter else block_ref[0]
    for copy in copies:
        copy.wait()


def exchange(blocks, axis, number, scatter):
    ranks = lax.axis_size(axis)
    return pl.pallas_call(
        lambda *refs: exchange_kernel(axis, ranks, scatter, *refs),
        name="exchange",
        in_specs=[pl.BlockSpec(memory_space=pltpu.VMEM)],
        out_specs=pl.BlockSpec(memory_space=pltpu.VMEM),
        out_shape=jax.ShapeDtypeStruct((ranks,) + blocks.shape[1:], blocks.dtype),
        scratch_shapes=[
            pltpu.SemaphoreType.DMA((ranks - 1,)),
            pltpu.SemaphoreType.DMA((ranks - 1,)),
        ],
        compiler_params=pltpu.CompilerParams(collective_id=number, has_side_effects=True),
        cost_estimate=pl.CostEstimate(
            flops=10_000_000_000, bytes_accessed=blocks.size * 4, transcendentals=0
        ),
    )(blocks)


def gather_rows(block, axis, number):
    got = exchange(block[None], axis, number, False)
    return got.reshape(-1, block.shape[1])


def scatter_sum(partial, axis, number):
    ranks = lax.axis_size(axis)
    got = exchange(partial.reshape(ranks, -1, partial.shape[1]), axis, number, True)
    return jnp.sum(got.astype(jnp.float32), axis=0)


def ring_position(index, size):
    if size % 2:
        return index
    side, line = index % 2, index // 2
    return line + side * (size - 1 - 2 * line)


def ring_index(position, size):
    if size % 2:
        return position
    side = position // (size // 2)
    line = position + side * (size - 1 - 2 * position)
    return line * 2 + side


def greet(peers):
    barrier = pltpu.get_barrier_semaphore()
    for target in peers:
        pl.semaphore_signal(
            barrier, inc=1, device_id=target, device_id_type=pl.DeviceIdType.MESH
        )
    pl.semaphore_wait(barrier, len(peers))


def send(source, place, sent, landed, target):
    copy = pltpu.make_async_remote_copy(
        src_ref=source,
        dst_ref=place,
        send_sem=sent,
        recv_sem=landed,
        device_id=target,
        device_id_type=pl.DeviceIdType.MESH,
    )
    copy.start()
    return copy


def others(axis):
    ranks = lax.axis_size(axis)
    mine = lax.axis_index(axis)
    return [lax.rem(mine + step, ranks) for step in range(1, ranks)]


def ring_ends(dp):
    at = ring_position(lax.axis_index("dp"), dp)
    after = ring_index((at + 1) % dp, dp)
    before = ring_index((at + dp - 1) % dp, dp)
    return at, after, before


def gather_kernel(dp, ranks, widths, count, *refs):
    parts = len(widths) + 1
    shards, rows = refs[:parts], refs[parts : parts + count]
    full_ref, small_ref = refs[parts + count : parts + count + 2]
    gots = refs[parts + count + 2 : parts + 2 * count + 2]
    own_sems, ring_sent, ring_got, row_sent, row_got = refs[parts + 2 * count + 2 :]
    me, mine = lax.axis_index("dp"), lax.axis_index("tensor")
    at, after, before = ring_ends(dp)
    peers = others("tensor")
    ends = [{"dp": after}, {"dp": before}]
    greet(ends + [{"tensor": peer} for peer in peers])
    lefts = [sum(widths[:part]) for part in range(parts)]
    hops = [[(dp - 1 + (part + way) % 2) // 2 for part in range(parts)] for way in range(2)]

    def place(owner, part):
        if part == parts - 1:
            return small_ref.at[owner]
        return full_ref.at[owner, :, pl.ds(lefts[part], widths[part])]

    flying = {}

    def hop(way, step, part):
        owner = ring_index((at + (dp - step if way == 0 else step)) % dp, dp)
        spot = place(owner, part)
        flying[way, step, part] = send(
            shards[part] if step == 0 else spot,
            spot,
            ring_sent.at[way, step, part],
            ring_got.at[way, step, part],
            ends[way],
        )

    for part in range(parts):
        for way in range(2):
            if hops[way][part] > 0:
                hop(way, 0, part)
    swaps = []
    for step, peer in enumerate(peers):
        for index in range(count):
            swaps.append(
                send(
                    rows[index],
                    gots[index].at[mine],
                    row_sent.at[step, index],
                    row_got.at[step, index],
                    {"tensor": peer},
                )
            )
    local = []
    for part in range(parts):
        local.append(pltpu.make_async_copy(shards[part], place(me, part), own_sems.at[part]))
    for index in range(count):
        local.append(
            pltpu.make_async_copy(rows[index], gots[index].at[mine], own_sems.at[parts + index])
        )
    for copy in local:
        copy.start()
    for step in range(1, max(max(line) for line in hops) + 1):
        for part in range(parts):
            for way in range(2):
                if hops[way][part] >= step:
                    flying[way, step - 1, part].wait_recv()
                    if hops[way][part] > step:
                        hop(way, step, part)
    for copy in local + swaps:
        copy.wait()
    for copy in flying.values():
        copy.wait_send()


def gather_all(shards, small, rows, number):
    dp, ranks = lax.axis_size("dp"), lax.axis_size("tensor")
    widths = [shard.shape[1] for shard in shards]
    parts, count = len(shards) + 1, len(rows)
    anywhere = pl.BlockSpec(memory_space=pl.ANY)
    vmem = pl.BlockSpec(memory_space=pltpu.VMEM)
    sem = pltpu.SemaphoreType.DMA
    got = pl.pallas_call(
        lambda *refs: gather_kernel(dp, ranks, widths, count, *refs),
        name="gather_all",
        in_specs=[anywhere] * (parts + count),
        out_specs=[vmem] * (2 + count),
        out_shape=[
            jax.ShapeDtypeStruct((dp, shards[0].shape[0], sum(widths)), shards[0].dtype),
            jax.ShapeDtypeStruct((dp,) + small.shape, small.dtype),
        ]
        + [jax.ShapeDtypeStruct((ranks,) + block.shape, block.dtype) for block in rows],
        scratch_shapes=[
            sem((parts + count,)),
            sem((2, max(1, dp // 2), parts)),
            sem((2, max(1, dp // 2), parts)),
            sem((ranks - 1, count)),
            sem((ranks - 1, count)),
        ],
        compiler_params=pltpu.CompilerParams(collective_id=number, has_side_effects=True),
        cost_estimate=pl.CostEstimate(
            flops=30_000_000_000, bytes_accessed=16_000_000, transcendentals=0
        ),
    )(*shards, small, *rows)
    full = got[0].reshape(-1, sum(widths))
    return full, got[1], [block.reshape(-1, block.shape[-1]) for block in got[2:]]


def reduce_kernel(dp, ranks, lines, count, *refs):
    arrays = count[0]
    grads, swaps_in, tile_ref = refs[:arrays], refs[arrays : arrays + count[1]], refs[arrays + count[1]]
    refs = refs[arrays + count[1] + 1 :]
    sums, swaps_out = refs[:arrays], refs[arrays : arrays + count[1]]
    tiles_ref, lines_ref = refs[arrays + count[1] : arrays + count[1] + 2]
    refs = refs[arrays + count[1] + 2 :]
    landed, totals = refs[:arrays], refs[arrays : 2 * arrays]
    ring_sent, ring_got, row_sent, row_got, tile_sent, tile_got, line_sent, line_got = refs[
        2 * arrays :
    ]
    me, mine = lax.axis_index("dp"), lax.axis_index("tensor")
    at, after, before = ring_ends(dp)
    peers, mates = others("tensor"), others("dp")
    ends = [{"dp": after}, {"dp": before}]
    greet([{"dp": mate} for mate in mates] + [{"tensor": peer} for peer in peers])
    last = dp - 2

    def owner(way, step):
        return ring_index((at + (2 * dp - 1 - step if way == 0 else 1 + step)) % dp, dp)

    flying = {}

    def hop(line, step):
        array, top, rows, way = lines[line]
        span = pl.ds(top, rows)
        source = grads[array].at[owner(way, 0), span] if step == 0 else totals[array].at[step - 1, span]
        flying[line, step] = send(
            source,
            landed[array].at[step, span],
            ring_sent.at[line, step],
            ring_got.at[line, step],
            ends[way],
        )

    for line in range(len(lines)):
        hop(line, 0)
    copies = []
    for step, mate in enumerate(mates):
        copies.append(
            send(tile_ref, tiles_ref.at[me], tile_sent.at[step], tile_got.at[step], {"dp": mate})
        )
    for index in range(count[1]):
        for step, peer in enumerate(peers):
            copies.append(
                send(
                    swaps_in[index].at[peer],
                    swaps_out[index].at[mine],
                    row_sent.at[step, index],
                    row_got.at[step, index],
                    {"tensor": peer},
                )
            )
    tiles_ref[me] = tile_ref[...]
    for index in range(count[1]):
        swaps_out[index][mine] = swaps_in[index][mine]
    for step in range(dp - 1):
        for line, (array, top, rows, way) in enumerate(lines):
            flying[line, step].wait_recv()
            span = pl.ds(top, rows)
            own = me if step == last else owner(way, step + 1)
            total = landed[array][step, span].astype(jnp.float32) + grads[array][
                own, span
            ].astype(jnp.float32)
            if step == last:
                sums[array][span] = total
            else:
                totals[array][step, span] = total.astype(totals[array].dtype)
                hop(line, step + 1)
    small = sums[arrays - 1]
    for step, peer in enumerate(peers):
        copies.append(
            send(small, lines_ref.at[mine], line_sent.at[step], line_got.at[step], {"tensor": peer})
        )
    lines_ref[mine] = small[...]
    for copy in copies:
        copy.wait()
    for copy in flying.values():
        copy.wait_send()


def reduce_all(grads, swaps, tile, number):
    dp, ranks = lax.axis_size("dp"), lax.axis_size("tensor")
    vmem = pl.BlockSpec(memory_space=pltpu.VMEM)
    sem = pltpu.SemaphoreType.DMA
    lines = []
    for array, grad in enumerate(grads):
        rows = grad.shape[1]
        pieces = 4 if rows * grad.shape[2] > 100_000 and rows % 64 == 0 else 2
        for piece in range(pieces):
            lines.append((array, piece * rows // pieces, rows // pieces, piece % 2))
    lines = lines[-2:] + lines[:-2]
    count = (len(grads), len(swaps))
    inputs = list(grads) + list(swaps) + [tile]
    small = grads[-1].shape[1:]
    results = pl.pallas_call(
        lambda *refs: reduce_kernel(dp, ranks, lines, count, *refs),
        name="reduce_all",
        in_specs=[vmem] * len(inputs),
        out_specs=[vmem] * (len(inputs) + 1),
        out_shape=[jax.ShapeDtypeStruct(grad.shape[1:], jnp.float32) for grad in grads]
        + [jax.ShapeDtypeStruct(block.shape, block.dtype) for block in swaps]
        + [
            jax.ShapeDtypeStruct((dp,) + tile.shape, tile.dtype),
            jax.ShapeDtypeStruct((ranks,) + small, jnp.float32),
        ],
        scratch_shapes=[pltpu.VMEM((dp - 1,) + grad.shape[1:], grad.dtype) for grad in grads]
        + [pltpu.VMEM((dp - 1,) + grad.shape[1:], grad.dtype) for grad in grads]
        + [
            sem((len(lines), dp - 1)),
            sem((len(lines), dp - 1)),
            sem((ranks - 1, len(swaps))),
            sem((ranks - 1, len(swaps))),
            sem((dp - 1,)),
            sem((dp - 1,)),
            sem((ranks - 1,)),
            sem((ranks - 1,)),
        ],
        compiler_params=pltpu.CompilerParams(collective_id=number, has_side_effects=True),
        cost_estimate=pl.CostEstimate(
            flops=30_000_000_000, bytes_accessed=16_000_000, transcendentals=0
        ),
    )(*inputs)
    arrays = len(grads)
    return results[:arrays], results[arrays : arrays + len(swaps)], results[-2], results[-1]


def short_conv(inputs, weights):
    tap_count = weights.shape[0]
    row_count = inputs.shape[0]
    padded = jnp.pad(inputs, ((tap_count - 1, 0), (0, 0)))
    result = jnp.zeros_like(inputs)
    for offset in range(tap_count):
        result = result + padded[offset : offset + row_count] * weights[offset]
    return result


def round_up(size, step):
    return -(-size // step) * step


def pad_columns(matrix_in, width):
    return jnp.pad(matrix_in, ((0, 0), (0, width - matrix_in.shape[1])))


def tap_rows(conv_weights):
    channels, heads, taps = conv_weights.shape
    return jnp.transpose(conv_weights, (1, 2, 0)).reshape(heads * taps, channels)


def joined_taps(rows, heads):
    shards, _, channels = rows.shape
    split = rows.reshape(shards, heads, -1, channels)
    taps = split.shape[2]
    return jnp.transpose(split, (2, 1, 0, 3)).reshape(taps, heads * shards * channels)


def split_taps(taps_in, heads, shards):
    taps, width = taps_in.shape
    split = taps_in.reshape(taps, heads, shards, width // (heads * shards))
    return jnp.transpose(split, (2, 1, 0, 3)).reshape(shards, heads * taps, -1)


def rate_terms(proj_beta, proj_alpha, log_rate, rate_bias):
    log_gates = -jnp.exp(log_rate) * jax.nn.softplus(proj_alpha + rate_bias)
    return jnp.concatenate([jax.nn.sigmoid(proj_beta), log_gates], axis=1)


def on_device(
    tokens, cotangent, norm1_gain, w_query, w_key, w_value, w_gate_out, w_out, w_beta, w_alpha,
    conv_query, conv_key, conv_value, a_log, dt_bias, head_gain, norm2_gain, w_up_gate, w_up,
    w_down,
):
    bf16, f32 = jnp.bfloat16, jnp.float32
    shard_rows, model = w_query.shape[0], tokens.shape[1]
    dp = model // shard_rows
    heads = a_log.shape[0]
    key_dim, value_dim = w_query.shape[1] // heads, w_value.shape[1] // heads
    taps = conv_query.shape[2]
    tap_lines = heads * taps
    qk_width, v_width = heads * key_dim, heads * value_dim
    conv_width = 2 * qk_width + v_width
    in_width = conv_width + v_width
    hidden_width = w_up.shape[1]
    ff = round_up(hidden_width, 256)

    packed = [tap_rows(conv_query), tap_rows(conv_key), tap_rows(conv_value), head_gain.T]
    lanes = [block.shape[1] for block in packed]
    lefts = [sum(lanes[:index]) for index in range(4)]
    line_rows = tap_lines + 2 + 2 * heads
    small_rows = round_up(line_rows, 16)
    small_width = round_up(max(sum(lanes), shard_rows), LANES)

    def small_block(groups, lines, kind):
        shards = groups[0].shape[0]
        group = jnp.concatenate(
            [jnp.pad(g, ((0, 0), (0, tap_lines - g.shape[1]), (0, 0))) for g in groups], axis=2
        )
        group = jnp.pad(group, ((0, 0), (0, 0), (0, small_width - sum(lanes))))
        lines = jnp.pad(lines, ((0, 0), (0, 0), (0, small_width - lines.shape[2])))
        rest = jnp.zeros((shards, small_rows - line_rows, small_width), kind)
        return jnp.concatenate([group.astype(kind), lines.astype(kind), rest], axis=1)

    small = small_block(
        [block[None] for block in packed],
        jnp.concatenate([norm1_gain[None], norm2_gain[None], w_beta.T, w_alpha.T], axis=0)[None],
        bf16,
    )[0]
    ffn_pack = jnp.concatenate([pad_columns(w, ff) for w in (w_up_gate, w_up, w_down)], axis=1)
    out_full = lax.all_gather(w_out, "dp", axis=0, tiled=True)
    out_full, ffn_pack = lax.optimization_barrier((out_full, ffn_pack))
    ffn_full = lax.all_gather(ffn_pack, "dp", axis=0, tiled=True)
    in_full, small_full, (tokens_got, cot_full) = gather_all(
        [w_query, w_key, w_value, w_gate_out], small, [tokens, cotangent], 1
    )
    small_all = small_full.astype(f32)

    def group_of(index, rows):
        return small_all[:, :rows, lefts[index] : lefts[index] + lanes[index]]

    def line_of(first, count):
        lines = small_all[:, tap_lines + first : tap_lines + first + count, :shard_rows]
        return jnp.swapaxes(lines, 0, 1).reshape(count, model)

    gain_one, gain_two = line_of(0, 1), line_of(1, 1)
    rate_weights = line_of(2, 2 * heads).astype(bf16)
    conv_weights = jnp.concatenate(
        [joined_taps(group_of(index, tap_lines), heads) for index in range(3)], axis=1
    )
    gain_row = joined_taps(group_of(3, heads), heads)

    tokens_full = tokens_got.astype(f32)
    _, unit_full = norm_forward(tokens_full)
    normed_one = (unit_full * gain_one).astype(bf16)
    projected = jnp.dot(normed_one, in_full, preferred_element_type=f32)
    proj_rates = times_transpose(normed_one, rate_weights)
    proj_conv = projected[:, :conv_width]
    proj_gate = projected[:, conv_width:]
    conv_all, conv_pull = jax.vjp(short_conv, proj_conv, conv_weights)
    rates, rates_pull = jax.vjp(
        rate_terms, proj_rates[:, :heads], proj_rates[:, heads:], a_log.astype(f32),
        dt_bias.astype(f32),
    )
    mixed, states, inverses = mixer_forward(
        conv_all, proj_gate, rates, gain_row, heads, key_dim, value_dim
    )
    row_values = tokens.astype(f32)
    scale_one, unit_one = norm_forward(row_values)
    middle = row_values + scatter_sum(
        times_transpose(mixed, out_full).astype(bf16), "tensor", 2
    )
    gates_full, down_full = ffn_full[:, : 2 * ff], ffn_full[:, 2 * ff :]
    scale_two, unit_two = norm_forward(middle)
    normed_two = gather_rows((unit_two * gain_two).astype(bf16), "tensor", 3)
    grad_hidden = jnp.dot(cot_full, down_full, preferred_element_type=f32)
    ups = jnp.dot(normed_two, gates_full, preferred_element_type=f32)
    up_gate, up_lin = ups[:, :ff], ups[:, ff:]
    gate_sigmoid = jax.nn.sigmoid(up_gate)
    hidden = (up_gate * gate_sigmoid * up_lin).astype(bf16)
    grad_gate = (
        grad_hidden * up_lin * gate_sigmoid * (1.0 + up_gate * (1.0 - gate_sigmoid))
    ).astype(bf16)
    grad_lin = (grad_hidden * up_gate * gate_sigmoid).astype(bf16)
    grad_ups = jnp.concatenate([grad_gate, grad_lin], axis=1)
    ffn_grads = jnp.concatenate(
        [
            weight_grad(normed_two, grad_ups).astype(bf16),
            weight_grad(cot_full, hidden).astype(bf16),
        ],
        axis=1,
    )
    grad_normed_part_two = times_transpose(grad_ups, gates_full).astype(bf16)
    grad_normed_part_two, ffn_grads = lax.optimization_barrier((grad_normed_part_two, ffn_grads))
    ffn_sums = lax.psum_scatter(ffn_grads, "dp", scatter_dimension=0, tiled=True)
    grad_normed_two = scatter_sum(grad_normed_part_two, "tensor", 4)
    grad_gain_two = jnp.sum(grad_normed_two * unit_two, axis=0)
    grad_middle = cotangent.astype(f32) + norm_backward(
        grad_normed_two, unit_two, scale_two, gain_two
    )
    mid_full = gather_rows(grad_middle.astype(bf16), "tensor", 5)
    ranks = lax.axis_size("tensor")
    out_grads = weight_grad(mid_full, mixed).astype(bf16)
    result_part = times_transpose(hidden, down_full).astype(bf16)

    grad_mixed = jnp.dot(mid_full, out_full, preferred_element_type=f32)
    grad_conv_all, grad_pgate, grad_rates, grad_gain_row = mixer_backward(
        conv_all, proj_gate, rates, gain_row, states, inverses, grad_mixed,
        heads, key_dim, value_dim,
    )
    grad_pconv, grad_conv_w = conv_pull(grad_conv_all)
    grad_beta, grad_alpha, grad_rate_part, grad_bias_part = rates_pull(grad_rates)
    grad_proj = jnp.concatenate([grad_pconv.astype(bf16), grad_pgate.astype(bf16)], axis=1)
    grad_rate_proj = jnp.concatenate([grad_beta, grad_alpha], axis=1).astype(bf16)
    grad_normed_part = times_transpose(grad_proj, in_full) + jnp.dot(
        grad_rate_proj, rate_weights, preferred_element_type=f32
    )
    grad_gain_one = jnp.sum(grad_normed_part * unit_full, axis=0)
    grad_lines = jnp.concatenate(
        [grad_gain_one[None], grad_gain_two[None], weight_grad(grad_rate_proj, normed_one)], axis=0
    )
    edges = [0, qk_width, 2 * qk_width, conv_width]
    grad_small = small_block(
        [split_taps(grad_conv_w[:, edges[i] : edges[i + 1]], heads, dp) for i in range(3)]
        + [split_taps(grad_gain_row, heads, dp)],
        jnp.swapaxes(grad_lines.reshape(2 + 2 * heads, dp, shard_rows), 0, 1),
        f32,
    )
    rate_line = jnp.concatenate([grad_rate_part, grad_bias_part])
    rate_tile = jnp.pad(rate_line[None], ((0, 7), (0, LANES - 2 * heads)))
    in_grads = weight_grad(normed_one, grad_proj).astype(bf16)
    sums, swapped, rate_tiles, small_lines = reduce_all(
        [
            in_grads.reshape(dp, shard_rows, in_width),
            out_grads.reshape(dp, shard_rows, v_width),
            grad_small,
        ],
        [
            grad_normed_part.astype(bf16).reshape(ranks, -1, model),
            result_part.reshape(ranks, -1, model),
        ],
        rate_tile,
        7,
    )
    in_sums, out_sums, small_sums = sums
    grad_normed_one = jnp.sum(swapped[0].astype(f32), axis=0)
    result = (middle + jnp.sum(swapped[1].astype(f32), axis=0)).astype(bf16)
    grad_rows = grad_middle + norm_backward(grad_normed_one, unit_one, scale_one, gain_one)
    rate_sums = jnp.sum(rate_tiles, axis=0)[0]
    gain_sums = jnp.sum(small_lines[:, tap_lines : tap_lines + 2, :shard_rows], axis=0)
    ffn_sums = ffn_sums.astype(f32)

    def taps_out(index, lines):
        block = small_sums[:lines, lefts[index] : lefts[index] + lanes[index]]
        return jnp.transpose(block.reshape(heads, -1, lanes[index]), (2, 0, 1))

    def lines_out(first):
        return small_sums[tap_lines + first : tap_lines + first + heads, :shard_rows].T

    return (
        result,
        grad_rows,
        gain_sums[0],
        in_sums[:, :qk_width],
        in_sums[:, qk_width : 2 * qk_width],
        in_sums[:, 2 * qk_width : conv_width],
        in_sums[:, conv_width:],
        out_sums,
        lines_out(2),
        lines_out(2 + heads),
        taps_out(0, tap_lines),
        taps_out(1, tap_lines),
        taps_out(2, tap_lines),
        rate_sums[:heads],
        rate_sums[heads : 2 * heads],
        taps_out(3, heads)[:, :, 0],
        gain_sums[1],
        ffn_sums[:, :hidden_width],
        ffn_sums[:, ff : ff + hidden_width],
        ffn_sums[:, 2 * ff : 2 * ff + hidden_width],
    )


def solution(mesh):
    placed = (
        P(("dp", "tensor"), None),
        P(("dp", "tensor"), None),
        P("dp"),
        P("dp", "tensor"),
        P("dp", "tensor"),
        P("dp", "tensor"),
        P("dp", "tensor"),
        P("dp", "tensor"),
        P("dp", "tensor"),
        P("dp", "tensor"),
        P("dp", "tensor", None),
        P("dp", "tensor", None),
        P("dp", "tensor", None),
        P("tensor"),
        P("tensor"),
        P("dp", "tensor"),
        P("dp"),
        P("dp", "tensor"),
        P("dp", "tensor"),
        P("dp", "tensor"),
    )
    return jax.shard_map(
        on_device,
        mesh=mesh,
        in_specs=placed,
        out_specs=(
            P(("dp", "tensor"), None),
            P(("dp", "tensor"), None),
            P("dp"),
            P("dp", "tensor"),
            P("dp", "tensor"),
            P("dp", "tensor"),
            P("dp", "tensor"),
            P("dp", "tensor"),
            P("dp", "tensor"),
            P("dp", "tensor"),
            P("dp", "tensor", None),
            P("dp", "tensor", None),
            P("dp", "tensor", None),
            P("tensor"),
            P("tensor"),
            P("dp", "tensor"),
            P("dp"),
            P("dp", "tensor"),
            P("dp", "tensor"),
            P("dp", "tensor"),
        ),
        check_vma=False,
    )
```

```python
import jax
import jax.numpy as jnp
from jax import lax
from jax.experimental import pallas as pl
from jax.experimental.pallas import tpu as pltpu
from jax.sharding import PartitionSpec as P

epsilon = 1e-06
CHUNK = 128
LANES = 128
contract_rows = (((0,), (0,)), ((), ()))
contract_cols = (((1,), (1,)), ((), ()))
contract_plain = (((1,), (0,)), ((), ()))
highest = lax.Precision.HIGHEST


def norm_forward(row_values):
    row_scale = lax.rsqrt(jnp.mean(row_values * row_values, axis=-1, keepdims=True) + epsilon)
    return (row_scale, row_values * row_scale)


def norm_backward(grad_normed, unit_values, row_scale, gain_values):
    grad_unit = grad_normed * gain_values
    return row_scale * (
        grad_unit - unit_values * jnp.mean(grad_unit * unit_values, axis=-1, keepdims=True)
    )


def weight_grad(left_in, right_in):
    return lax.dot_general(left_in, right_in, contract_rows, preferred_element_type=jnp.float32)


def times_transpose(left_in, right_in):
    return lax.dot_general(left_in, right_in, contract_cols, preferred_element_type=jnp.float32)


def fine_dot(left_in, right_in, dims=contract_plain):
    return lax.dot_general(
        left_in, right_in, dims, precision=lax.Precision.HIGH, preferred_element_type=jnp.float32
    )


def exact_dot(left_in, right_in, dims=contract_plain):
    return fine_dot(left_in, right_in, dims)


def silu(values):
    return values * lax.logistic(values)


def unit_length(values):
    return values * lax.rsqrt(jnp.sum(values * values, axis=-1, keepdims=True) + epsilon)


def triangle_masks(size):
    row = lax.broadcasted_iota(jnp.int32, (size, size), 0)
    col = lax.broadcasted_iota(jnp.int32, (size, size), 1)
    return row, col


def unit_lower_inverses(lowers):
    size = lowers[0].shape[0]
    row, col = triangle_masks(size)
    eye = jnp.where(row == col, 1.0, 0.0)
    inverses = [eye for _ in lowers]
    bit = 0
    while (1 << bit) < size:
        joined = ((row >> (bit + 1)) == (col >> (bit + 1))) & ((row >> bit) != (col >> bit))
        parts = [jnp.where(joined, lower, 0.0) for lower in lowers]
        if bit == 0:
            inverses = [eye - part for part in parts]
        else:
            inner = [fine_dot(part, inverse) for part, inverse in zip(parts, inverses)]
            steps = [fine_dot(inverse, step) for inverse, step in zip(inverses, inner)]
            inverses = [inverse - step for inverse, step in zip(inverses, steps)]
        bit += 1
    return inverses


@jax.custom_vjp
def known_inverse(lower, inverse):
    return inverse


def known_inverse_fwd(lower, inverse):
    return inverse, inverse


def known_inverse_bwd(inverse, grad):
    turned = inverse.T
    return -fine_dot(fine_dot(turned, grad), turned), jnp.zeros_like(inverse)


known_inverse.defvjp(known_inverse_fwd, known_inverse_bwd)


def each(call, *lists):
    return [call(*items) for items in zip(*lists)]


def mixer_chunk(conv_q, conv_k, conv_v, proj_gate, beta, gate, gain, state, inverter):
    size, key_dim = conv_q[0].shape
    row, col = triangle_masks(size)
    strict = row > col
    lower = row >= col
    query = each(lambda v: unit_length(silu(v)) * key_dim ** (-0.5), conv_q)
    key = each(lambda v: unit_length(silu(v)), conv_k)
    value = each(silu, conv_v)
    wide = each(lambda g: jnp.broadcast_to(g, (size, size)), gate)
    decay_col = each(
        lambda w: jnp.sum(jnp.where(lower, w.T, 0.0), axis=1, keepdims=True), wide
    )
    decay_row = each(
        lambda w: jnp.sum(jnp.where(row <= col, w, 0.0), axis=0, keepdims=True), wide
    )
    decay_end = each(lambda g: jnp.sum(g, axis=0, keepdims=True), gate)
    differ = each(lambda c, r: jnp.where(strict, c - r, 0.0), decay_col, decay_row)
    decay = each(lambda d: jnp.where(lower, jnp.exp(d), 0.0), differ)
    grams = each(lambda k: exact_dot(k, k, contract_cols), key)
    system = each(lambda g, d, b: jnp.where(strict, g * d * b, 0.0), grams, decay, beta)
    inverse = inverter(system)
    grown = each(jnp.exp, decay_col)
    kept = each(lambda k, b, g, s: exact_dot(k * (b * g), s), key, beta, grown, state)
    fresh = each(lambda i, v, b, k: exact_dot(i, v * b - k), inverse, value, beta, kept)
    scores = each(lambda q, k, d: exact_dot(q, k, contract_cols) * d, query, key, decay)
    carried = each(lambda q, g, s: exact_dot(q * g, s), query, grown, state)
    mixed = each(lambda c, s, f: c + exact_dot(s, f), carried, scores, fresh)
    added = each(
        lambda k, e, c, f: exact_dot(k * jnp.exp(e - c), f, contract_rows),
        key, decay_end, decay_col, fresh,
    )
    new_state = each(lambda e, s, a: jnp.exp(e) * s + a, decay_end, state, added)
    gated = each(
        lambda m, g, p: m
        * lax.rsqrt(jnp.mean(m * m, axis=-1, keepdims=True) + epsilon)
        * g
        * silu(p),
        mixed, gain, proj_gate,
    )
    return gated, new_state, inverse


def head_slices(head, heads, key_dim, value_dim):
    q_at = head * key_dim
    k_at = (heads + head) * key_dim
    v_at = 2 * heads * key_dim + head * value_dim
    return (
        slice(q_at, q_at + key_dim),
        slice(k_at, k_at + key_dim),
        slice(v_at, v_at + value_dim),
        slice(head * value_dim, (head + 1) * value_dim),
    )


def head_inputs(heads, key_dim, value_dim, conv_ref, pgate_ref, rates_ref, gain_ref):
    at = [head_slices(head, heads, key_dim, value_dim) for head in range(heads)]
    return at, (
        [conv_ref[:, spots[0]] for spots in at],
        [conv_ref[:, spots[1]] for spots in at],
        [conv_ref[:, spots[2]] for spots in at],
        [pgate_ref[:, spots[3]] for spots in at],
        [rates_ref[:, head : head + 1] for head in range(heads)],
        [rates_ref[:, heads + head : heads + head + 1] for head in range(heads)],
        [gain_ref[:, spots[3]] for spots in at],
    )


def mixer_forward_kernel(
    heads, key_dim, value_dim, conv_ref, pgate_ref, rates_ref, gain_ref,
    gated_ref, states_ref, inverses_ref, state_ref,
):
    @pl.when(pl.program_id(0) == 0)
    def _():
        state_ref[...] = jnp.zeros_like(state_ref)

    at, operands = head_inputs(
        heads, key_dim, value_dim, conv_ref, pgate_ref, rates_ref, gain_ref
    )
    state = [state_ref[head] for head in range(heads)]
    gated, new_state, inverse = mixer_chunk(*operands, state, unit_lower_inverses)
    for head in range(heads):
        gated_ref[:, at[head][3]] = gated[head].astype(gated_ref.dtype)
        states_ref[0, head] = state[head]
        inverses_ref[0, head] = inverse[head]
        state_ref[head] = new_state[head]


def mixer_backward_kernel(
    heads, key_dim, value_dim, conv_ref, pgate_ref, rates_ref, gain_ref, states_ref,
    inverses_ref, grad_ref, gconv_ref, gpgate_ref, grates_ref, ggain_ref, gstate_ref,
):
    @pl.when(pl.program_id(0) == 0)
    def _():
        gstate_ref[...] = jnp.zeros_like(gstate_ref)
        ggain_ref[...] = jnp.zeros_like(ggain_ref)

    lane = lax.broadcasted_iota(jnp.int32, grates_ref.shape, 1)
    rates_grad = jnp.zeros(grates_ref.shape, jnp.float32)
    at, operands = head_inputs(
        heads, key_dim, value_dim, conv_ref, pgate_ref, rates_ref, gain_ref
    )
    inverses = [inverses_ref[0, head] for head in range(heads)]

    def run(*operands):
        gated, new_state, _ = mixer_chunk(
            *operands, lambda systems: each(known_inverse, systems, inverses)
        )
        return gated, new_state

    _, pull = jax.vjp(run, *operands, [states_ref[0, head] for head in range(heads)])
    pulled = pull(
        (
            [grad_ref[:, spots[3]] for spots in at],
            [gstate_ref[head] for head in range(heads)],
        )
    )
    for head in range(heads):
        at_q, at_k, at_v, at_g = at[head]
        gconv_ref[:, at_q] = pulled[0][head]
        gconv_ref[:, at_k] = pulled[1][head]
        gconv_ref[:, at_v] = pulled[2][head]
        gpgate_ref[:, at_g] = pulled[3][head]
        rates_grad = jnp.where(lane == head, pulled[4][head], rates_grad)
        rates_grad = jnp.where(lane == heads + head, pulled[5][head], rates_grad)
        ggain_ref[:, at_g] += pulled[6][head]
        gstate_ref[head] = pulled[7][head]
    grates_ref[...] = rates_grad


def row_block(width, order):
    return pl.BlockSpec((CHUNK, width), lambda step: (order(step), 0))


def mixer_forward(conv_all, proj_gate, rates, gain_row, heads, key_dim, value_dim):
    rows, conv_width = conv_all.shape
    steps = rows // CHUNK
    forward = lambda step: step
    width = heads * value_dim
    return pl.pallas_call(
        lambda *refs: mixer_forward_kernel(heads, key_dim, value_dim, *refs),
        name="mixer_forward",
        grid=(steps,),
        in_specs=[
            row_block(conv_width, forward),
            row_block(width, forward),
            row_block(rates.shape[1], forward),
            pl.BlockSpec((1, width), lambda step: (0, 0)),
        ],
        out_specs=[
            row_block(width, forward),
            pl.BlockSpec((1, heads, key_dim, value_dim), lambda step: (step, 0, 0, 0)),
            pl.BlockSpec((1, heads, CHUNK, CHUNK), lambda step: (step, 0, 0, 0)),
        ],
        out_shape=[
            jax.ShapeDtypeStruct((rows, width), jnp.bfloat16),
            jax.ShapeDtypeStruct((steps, heads, key_dim, value_dim), jnp.float32),
            jax.ShapeDtypeStruct((steps, heads, CHUNK, CHUNK), jnp.float32),
        ],
        scratch_shapes=[pltpu.VMEM((heads, key_dim, value_dim), jnp.float32)],
        cost_estimate=pl.CostEstimate(
            flops=30_000_000_000, bytes_accessed=8_000_000, transcendentals=1_000_000
        ),
    )(conv_all, proj_gate, rates, gain_row)


def mixer_backward(
    conv_all, proj_gate, rates, gain_row, states, inverses, grad_gated, heads, key_dim, value_dim
):
    rows, conv_width = conv_all.shape
    steps = rows // CHUNK
    back = lambda step: steps - 1 - step
    width = heads * value_dim
    return pl.pallas_call(
        lambda *refs: mixer_backward_kernel(heads, key_dim, value_dim, *refs),
        name="mixer_backward",
        grid=(steps,),
        in_specs=[
            row_block(conv_width, back),
            row_block(width, back),
            row_block(rates.shape[1], back),
            pl.BlockSpec((1, width), lambda step: (0, 0)),
            pl.BlockSpec((1, heads, key_dim, value_dim), lambda step: (back(step), 0, 0, 0)),
            pl.BlockSpec((1, heads, CHUNK, CHUNK), lambda step: (back(step), 0, 0, 0)),
            row_block(width, back),
        ],
        out_specs=[
            row_block(conv_width, back),
            row_block(width, back),
            row_block(rates.shape[1], back),
            pl.BlockSpec((1, width), lambda step: (0, 0)),
        ],
        out_shape=[
            jax.ShapeDtypeStruct((rows, conv_width), jnp.float32),
            jax.ShapeDtypeStruct((rows, width), jnp.float32),
            jax.ShapeDtypeStruct(rates.shape, jnp.float32),
            jax.ShapeDtypeStruct((1, width), jnp.float32),
        ],
        scratch_shapes=[pltpu.VMEM((heads, key_dim, value_dim), jnp.float32)],
        cost_estimate=pl.CostEstimate(
            flops=30_000_000_000, bytes_accessed=12_000_000, transcendentals=2_000_000
        ),
    )(conv_all, proj_gate, rates, gain_row, states, inverses, grad_gated)


def ring_position(index, size):
    if size % 2:
        return index
    side, line = index % 2, index // 2
    return line + side * (size - 1 - 2 * line)


def ring_index(position, size):
    if size % 2:
        return position
    side = position // (size // 2)
    line = position + side * (size - 1 - 2 * position)
    return line * 2 + side


def greet(peers):
    barrier = pltpu.get_barrier_semaphore()
    for target in peers:
        pl.semaphore_signal(
            barrier, inc=1, device_id=target, device_id_type=pl.DeviceIdType.MESH
        )
    pl.semaphore_wait(barrier, len(peers))


def send(source, place, sent, landed, target):
    copy = pltpu.make_async_remote_copy(
        src_ref=source,
        dst_ref=place,
        send_sem=sent,
        recv_sem=landed,
        device_id=target,
        device_id_type=pl.DeviceIdType.MESH,
    )
    copy.start()
    return copy


def others(axis):
    ranks = lax.axis_size(axis)
    mine = lax.axis_index(axis)
    return [lax.rem(mine + step, ranks) for step in range(1, ranks)]


def ring_ends(dp):
    at = ring_position(lax.axis_index("dp"), dp)
    after = ring_index((at + 1) % dp, dp)
    before = ring_index((at + dp - 1) % dp, dp)
    return at, after, before


def gather_kernel(dp, ranks, widths, count, *refs):
    parts = len(widths) + 1
    shards, rows = refs[:parts], refs[parts : parts + count]
    full_ref, small_ref = refs[parts + count : parts + count + 2]
    gots = refs[parts + count + 2 : parts + 2 * count + 2]
    own_sems, ring_sent, ring_got, row_sent, row_got = refs[parts + 2 * count + 2 :]
    me, mine = lax.axis_index("dp"), lax.axis_index("tensor")
    at, after, before = ring_ends(dp)
    peers = others("tensor")
    ends = [{"dp": after}, {"dp": before}]
    greet(ends + [{"tensor": peer} for peer in peers])
    lefts = [sum(widths[:part]) for part in range(parts)]
    hops = [[(dp - 1 + (part + way) % 2) // 2 for part in range(parts)] for way in range(2)]

    def place(owner, part):
        if part == parts - 1:
            return small_ref.at[owner]
        return full_ref.at[owner, :, pl.ds(lefts[part], widths[part])]

    flying = {}

    def hop(way, step, part):
        owner = ring_index((at + (dp - step if way == 0 else step)) % dp, dp)
        spot = place(owner, part)
        flying[way, step, part] = send(
            shards[part] if step == 0 else spot,
            spot,
            ring_sent.at[way, step, part],
            ring_got.at[way, step, part],
            ends[way],
        )

    for part in range(parts):
        for way in range(2):
            if hops[way][part] > 0:
                hop(way, 0, part)
    swaps = []
    for step, peer in enumerate(peers):
        for index in range(count):
            swaps.append(
                send(
                    rows[index],
                    gots[index].at[mine],
                    row_sent.at[step, index],
                    row_got.at[step, index],
                    {"tensor": peer},
                )
            )
    local = []
    for part in range(parts):
        local.append(pltpu.make_async_copy(shards[part], place(me, part), own_sems.at[part]))
    for index in range(count):
        local.append(
            pltpu.make_async_copy(rows[index], gots[index].at[mine], own_sems.at[parts + index])
        )
    for copy in local:
        copy.start()
    for step in range(1, max(max(line) for line in hops) + 1):
        for part in range(parts):
            for way in range(2):
                if hops[way][part] >= step:
                    flying[way, step - 1, part].wait_recv()
                    if hops[way][part] > step:
                        hop(way, step, part)
    for copy in local + swaps:
        copy.wait()
    for copy in flying.values():
        copy.wait_send()


def gather_all(shards, small, rows, number):
    dp, ranks = lax.axis_size("dp"), lax.axis_size("tensor")
    widths = [shard.shape[1] for shard in shards]
    parts, count = len(shards) + 1, len(rows)
    anywhere = pl.BlockSpec(memory_space=pl.ANY)
    vmem = pl.BlockSpec(memory_space=pltpu.VMEM)
    sem = pltpu.SemaphoreType.DMA
    got = pl.pallas_call(
        lambda *refs: gather_kernel(dp, ranks, widths, count, *refs),
        name="gather_all",
        in_specs=[anywhere] * (parts + count),
        out_specs=[vmem] * (2 + count),
        out_shape=[
            jax.ShapeDtypeStruct((dp, shards[0].shape[0], sum(widths)), shards[0].dtype),
            jax.ShapeDtypeStruct((dp,) + small.shape, small.dtype),
        ]
        + [jax.ShapeDtypeStruct((ranks,) + block.shape, block.dtype) for block in rows],
        scratch_shapes=[
            sem((parts + count,)),
            sem((2, max(1, dp // 2), parts)),
            sem((2, max(1, dp // 2), parts)),
            sem((ranks - 1, count)),
            sem((ranks - 1, count)),
        ],
        compiler_params=pltpu.CompilerParams(collective_id=number, has_side_effects=True),
        cost_estimate=pl.CostEstimate(
            flops=30_000_000_000, bytes_accessed=16_000_000, transcendentals=0
        ),
    )(*shards, small, *rows)
    full = got[0].reshape(-1, sum(widths))
    return full, got[1], [block.reshape(-1, block.shape[-1]) for block in got[2:]]


def reduce_kernel(dp, ranks, lines, count, *refs):
    arrays = count[0]
    grads, swaps_in, tile_ref = refs[:arrays], refs[arrays : arrays + count[1]], refs[arrays + count[1]]
    refs = refs[arrays + count[1] + 1 :]
    sums, swaps_out = refs[:arrays], refs[arrays : arrays + count[1]]
    tiles_ref, lines_ref = refs[arrays + count[1] : arrays + count[1] + 2]
    refs = refs[arrays + count[1] + 2 :]
    landed, totals = refs[:arrays], refs[arrays : 2 * arrays]
    ring_sent, ring_got, row_sent, row_got, tile_sent, tile_got, line_sent, line_got = refs[
        2 * arrays :
    ]
    me, mine = lax.axis_index("dp"), lax.axis_index("tensor")
    at, after, before = ring_ends(dp)
    peers, mates = others("tensor"), others("dp")
    ends = [{"dp": after}, {"dp": before}]
    greet([{"dp": mate} for mate in mates] + [{"tensor": peer} for peer in peers])
    last = dp - 2

    def owner(way, step):
        return ring_index((at + (2 * dp - 1 - step if way == 0 else 1 + step)) % dp, dp)

    flying = {}

    def hop(line, step):
        array, top, rows, way = lines[line]
        span = pl.ds(top, rows)
        source = grads[array].at[owner(way, 0), span] if step == 0 else totals[array].at[step - 1, span]
        flying[line, step] = send(
            source,
            landed[array].at[step, span],
            ring_sent.at[line, step],
            ring_got.at[line, step],
            ends[way],
        )

    for line in range(len(lines)):
        hop(line, 0)
    copies = []
    for step, mate in enumerate(mates):
        copies.append(
            send(tile_ref, tiles_ref.at[me], tile_sent.at[step], tile_got.at[step], {"dp": mate})
        )
    for index in range(count[1]):
        for step, peer in enumerate(peers):
            copies.append(
                send(
                    swaps_in[index].at[peer],
                    swaps_out[index].at[mine],
                    row_sent.at[step, index],
                    row_got.at[step, index],
                    {"tensor": peer},
                )
            )
    tiles_ref[me] = tile_ref[...]
    for index in range(count[1]):
        swaps_out[index][mine] = swaps_in[index][mine]
    for step in range(dp - 1):
        for line, (array, top, rows, way) in enumerate(lines):
            flying[line, step].wait_recv()
            span = pl.ds(top, rows)
            own = me if step == last else owner(way, step + 1)
            total = landed[array][step, span].astype(jnp.float32) + grads[array][
                own, span
            ].astype(jnp.float32)
            if step == last:
                sums[array][span] = total
            else:
                totals[array][step, span] = total.astype(totals[array].dtype)
                hop(line, step + 1)
    small = sums[arrays - 1]
    for step, peer in enumerate(peers):
        copies.append(
            send(small, lines_ref.at[mine], line_sent.at[step], line_got.at[step], {"tensor": peer})
        )
    lines_ref[mine] = small[...]
    for copy in copies:
        copy.wait()
    for copy in flying.values():
        copy.wait_send()


def reduce_all(grads, swaps, tile, number):
    dp, ranks = lax.axis_size("dp"), lax.axis_size("tensor")
    vmem = pl.BlockSpec(memory_space=pltpu.VMEM)
    sem = pltpu.SemaphoreType.DMA
    lines = []
    for array, grad in enumerate(grads):
        rows = grad.shape[1]
        pieces = 4 if rows * grad.shape[2] > 100_000 and rows % 64 == 0 else 2
        for piece in range(pieces):
            lines.append((array, piece * rows // pieces, rows // pieces, piece % 2))
    lines = lines[-2:] + lines[:-2]
    count = (len(grads), len(swaps))
    inputs = list(grads) + list(swaps) + [tile]
    small = grads[-1].shape[1:]
    results = pl.pallas_call(
        lambda *refs: reduce_kernel(dp, ranks, lines, count, *refs),
        name="reduce_all",
        in_specs=[vmem] * len(inputs),
        out_specs=[vmem] * (len(inputs) + 1),
        out_shape=[jax.ShapeDtypeStruct(grad.shape[1:], jnp.float32) for grad in grads]
        + [jax.ShapeDtypeStruct(block.shape, block.dtype) for block in swaps]
        + [
            jax.ShapeDtypeStruct((dp,) + tile.shape, tile.dtype),
            jax.ShapeDtypeStruct((ranks,) + small, jnp.float32),
        ],
        scratch_shapes=[pltpu.VMEM((dp - 1,) + grad.shape[1:], grad.dtype) for grad in grads]
        + [pltpu.VMEM((dp - 1,) + grad.shape[1:], grad.dtype) for grad in grads]
        + [
            sem((len(lines), dp - 1)),
            sem((len(lines), dp - 1)),
            sem((ranks - 1, len(swaps))),
            sem((ranks - 1, len(swaps))),
            sem((dp - 1,)),
            sem((dp - 1,)),
            sem((ranks - 1,)),
            sem((ranks - 1,)),
        ],
        compiler_params=pltpu.CompilerParams(collective_id=number, has_side_effects=True),
        cost_estimate=pl.CostEstimate(
            flops=30_000_000_000, bytes_accessed=16_000_000, transcendentals=0
        ),
    )(*inputs)
    arrays = len(grads)
    return results[:arrays], results[arrays : arrays + len(swaps)], results[-2], results[-1]


def forward_finish(summed, tokens_ref, gain_ref, middle_ref, span):
    middle = tokens_ref[span].astype(jnp.float32) + summed
    middle_ref[span] = middle
    _, unit = norm_forward(middle)
    return unit * gain_ref[...]


def backward_finish(summed, cotangent_ref, gain_ref, middle_ref, grad_ref, gain_grad_ref, span):
    scale, unit = norm_forward(middle_ref[span])
    gain_grad_ref[...] += jnp.sum(summed * unit, axis=0, keepdims=True)
    grad = cotangent_ref[span].astype(jnp.float32) + norm_backward(
        summed, unit, scale, gain_ref[...]
    )
    grad_ref[span] = grad
    return grad


def turn_kernel(ranks, chunks, backward, *refs):
    if backward:
        part_ref, rows_ref, gain_ref, middle_ref, got_ref, grad_ref, gain_grad_ref = refs[:7]
        scratch = refs[7:]
        gain_grad_ref[...] = jnp.zeros_like(gain_grad_ref)
    else:
        part_ref, rows_ref, gain_ref, got_ref, middle_ref = refs[:5]
        scratch = refs[5:]
    pair_buf, sum_buf, far_buf, pair_s, pair_r, far_s, far_r, out_s, out_r, on_s, on_r = scratch
    mine = lax.axis_index("tensor")
    side, group = mine % 2, mine // 2
    groups = ranks // 2
    partner = group * 2 + 1 - side
    away = [(group + step) % groups for step in range(1, groups)]
    mates = [{"tensor": other * 2 + side} for other in away]
    near = {"tensor": partner}
    greet([near] + mates)
    rows = part_ref.shape[1] // chunks
    flying = []
    spans = [pl.ds(chunk * rows, rows) for chunk in range(chunks)]

    def go(*operands):
        copy = send(*operands)
        flying.append(copy)
        return copy

    pairs, fars, outs, ons, backs = {}, {}, {}, {}, {}
    order = away + [group]
    for chunk, span in enumerate(spans):
        for step, other in enumerate(order):
            pairs[step, chunk] = go(
                part_ref.at[other * 2 + 1 - side, span],
                pair_buf.at[step, span],
                pair_s.at[step, chunk],
                pair_r.at[step, chunk],
                near,
            )
    for chunk, span in enumerate(spans):
        for step, other in enumerate(away):
            pairs[step, chunk].wait_recv()
            total = part_ref[other * 2 + side, span].astype(jnp.float32) + pair_buf[
                step, span
            ].astype(jnp.float32)
            sum_buf[step, span] = total.astype(sum_buf.dtype)
            fars[step, chunk] = go(
                sum_buf.at[step, span],
                far_buf.at[step, span],
                far_s.at[step, chunk],
                far_r.at[step, chunk],
                mates[step],
            )
    for chunk, span in enumerate(spans):
        pairs[groups - 1, chunk].wait_recv()
        summed = part_ref[mine, span].astype(jnp.float32) + pair_buf[groups - 1, span].astype(
            jnp.float32
        )
        for step in range(groups - 1):
            fars[step, chunk].wait_recv()
            summed = summed + far_buf[step, span].astype(jnp.float32)
        if backward:
            done = backward_finish(
                summed, rows_ref, gain_ref, middle_ref, grad_ref, gain_grad_ref, span
            )
        else:
            done = forward_finish(summed, rows_ref, gain_ref, middle_ref, span)
        got_ref[mine, span] = done.astype(got_ref.dtype)
        place = got_ref.at[mine, span]
        for step in range(groups - 1):
            outs[step, chunk] = go(
                place, place, out_s.at[step, chunk], out_r.at[step, chunk], mates[step]
            )
        ons[groups - 1, chunk] = go(
            place, place, on_s.at[groups - 1, chunk], on_r.at[groups - 1, chunk], near
        )
    for chunk, span in enumerate(spans):
        for step in range(groups - 1):
            outs[step, chunk].wait_recv()
            source = ((group + groups - 1 - step) % groups) * 2 + side
            place = got_ref.at[source, span]
            ons[step, chunk] = go(
                place, place, on_s.at[step, chunk], on_r.at[step, chunk], near
            )
    for chunk in range(chunks):
        for step in range(groups):
            ons[step, chunk].wait_recv()
    for copy in flying:
        copy.wait_send()


def turn(part, own_rows, gain, number, middle=None, chunks=4):
    ranks = lax.axis_size("tensor")
    rows, model = own_rows.shape
    chunks = chunks if rows % (16 * chunks) == 0 else 1
    groups = ranks // 2
    backward = middle is not None
    vmem = pl.BlockSpec(memory_space=pltpu.VMEM)
    sem = pltpu.SemaphoreType.DMA
    out_shape = [
        jax.ShapeDtypeStruct((ranks, rows, model), jnp.bfloat16),
        jax.ShapeDtypeStruct((rows, model), jnp.float32),
    ]
    inputs = [part.reshape(ranks, rows, model), own_rows, gain]
    if backward:
        out_shape.append(jax.ShapeDtypeStruct((1, model), jnp.float32))
        inputs.append(middle)
    results = pl.pallas_call(
        lambda *refs: turn_kernel(ranks, chunks, backward, *refs),
        name="turn_backward" if backward else "turn_forward",
        in_specs=[vmem] * len(inputs),
        out_specs=[vmem] * len(out_shape),
        out_shape=out_shape,
        scratch_shapes=[
            pltpu.VMEM((groups, rows, model), jnp.bfloat16),
            pltpu.VMEM((max(1, groups - 1), rows, model), jnp.bfloat16),
            pltpu.VMEM((max(1, groups - 1), rows, model), jnp.bfloat16),
        ]
        + [sem((groups, chunks))] * 8,
        compiler_params=pltpu.CompilerParams(collective_id=number, has_side_effects=True),
        cost_estimate=pl.CostEstimate(
            flops=10_000_000_000, bytes_accessed=4_000_000, transcendentals=0
        ),
    )(*inputs)
    return (results[0].reshape(-1, model),) + tuple(results[1:])


def short_conv(inputs, weights):
    tap_count = weights.shape[0]
    row_count = inputs.shape[0]
    padded = jnp.pad(inputs, ((tap_count - 1, 0), (0, 0)))
    result = jnp.zeros_like(inputs)
    for offset in range(tap_count):
        result = result + padded[offset : offset + row_count] * weights[offset]
    return result


def round_up(size, step):
    return -(-size // step) * step


def pad_columns(matrix_in, width):
    return jnp.pad(matrix_in, ((0, 0), (0, width - matrix_in.shape[1])))


def tap_rows(conv_weights):
    channels, heads, taps = conv_weights.shape
    return jnp.transpose(conv_weights, (1, 2, 0)).reshape(heads * taps, channels)


def joined_taps(rows, heads):
    shards, _, channels = rows.shape
    split = rows.reshape(shards, heads, -1, channels)
    taps = split.shape[2]
    return jnp.transpose(split, (2, 1, 0, 3)).reshape(taps, heads * shards * channels)


def split_taps(taps_in, heads, shards):
    taps, width = taps_in.shape
    split = taps_in.reshape(taps, heads, shards, width // (heads * shards))
    return jnp.transpose(split, (2, 1, 0, 3)).reshape(shards, heads * taps, -1)


def rate_terms(proj_beta, proj_alpha, log_rate, rate_bias):
    log_gates = -jnp.exp(log_rate) * jax.nn.softplus(proj_alpha + rate_bias)
    return jnp.concatenate([jax.nn.sigmoid(proj_beta), log_gates], axis=1)


def on_device(
    tokens, cotangent, norm1_gain, w_query, w_key, w_value, w_gate_out, w_out, w_beta, w_alpha,
    conv_query, conv_key, conv_value, a_log, dt_bias, head_gain, norm2_gain, w_up_gate, w_up,
    w_down,
):
    bf16, f32 = jnp.bfloat16, jnp.float32
    shard_rows, model = w_query.shape[0], tokens.shape[1]
    dp = model // shard_rows
    heads = a_log.shape[0]
    key_dim, value_dim = w_query.shape[1] // heads, w_value.shape[1] // heads
    taps = conv_query.shape[2]
    tap_lines = heads * taps
    qk_width, v_width = heads * key_dim, heads * value_dim
    conv_width = 2 * qk_width + v_width
    in_width = conv_width + v_width
    hidden_width = w_up.shape[1]
    ff = round_up(hidden_width, 256)

    packed = [tap_rows(conv_query), tap_rows(conv_key), tap_rows(conv_value), head_gain.T]
    lanes = [block.shape[1] for block in packed]
    lefts = [sum(lanes[:index]) for index in range(4)]
    line_rows = tap_lines + 2 + 2 * heads
    small_rows = round_up(line_rows, 16)
    small_width = round_up(max(sum(lanes), shard_rows), LANES)

    def small_block(groups, lines, kind):
        shards = groups[0].shape[0]
        group = jnp.concatenate(
            [jnp.pad(g, ((0, 0), (0, tap_lines - g.shape[1]), (0, 0))) for g in groups], axis=2
        )
        group = jnp.pad(group, ((0, 0), (0, 0), (0, small_width - sum(lanes))))
        lines = jnp.pad(lines, ((0, 0), (0, 0), (0, small_width - lines.shape[2])))
        rest = jnp.zeros((shards, small_rows - line_rows, small_width), kind)
        return jnp.concatenate([group.astype(kind), lines.astype(kind), rest], axis=1)

    small = small_block(
        [block[None] for block in packed],
        jnp.concatenate([norm1_gain[None], norm2_gain[None], w_beta.T, w_alpha.T], axis=0)[None],
        bf16,
    )[0]
    ffn_pack = jnp.concatenate([pad_columns(w, ff) for w in (w_up_gate, w_up, w_down)], axis=1)
    out_full = lax.all_gather(w_out, "dp", axis=0, tiled=True)
    out_full, ffn_pack = lax.optimization_barrier((out_full, ffn_pack))
    ffn_full = lax.all_gather(ffn_pack, "dp", axis=0, tiled=True)
    in_full, small_full, (tokens_got, cot_full) = gather_all(
        [w_query, w_key, w_value, w_gate_out], small, [tokens, cotangent], 1
    )
    small_all = small_full.astype(f32)

    def group_of(index, rows):
        return small_all[:, :rows, lefts[index] : lefts[index] + lanes[index]]

    def line_of(first, count):
        lines = small_all[:, tap_lines + first : tap_lines + first + count, :shard_rows]
        return jnp.swapaxes(lines, 0, 1).reshape(count, model)

    gain_one, gain_two = line_of(0, 1), line_of(1, 1)
    rate_weights = line_of(2, 2 * heads).astype(bf16)
    conv_weights = jnp.concatenate(
        [joined_taps(group_of(index, tap_lines), heads) for index in range(3)], axis=1
    )
    gain_row = joined_taps(group_of(3, heads), heads)

    tokens_full = tokens_got.astype(f32)
    _, unit_full = norm_forward(tokens_full)
    normed_one = (unit_full * gain_one).astype(bf16)
    projected = jnp.dot(normed_one, in_full, preferred_element_type=f32)
    proj_rates = times_transpose(normed_one, rate_weights)
    proj_conv = projected[:, :conv_width]
    proj_gate = projected[:, conv_width:]
    conv_all, conv_pull = jax.vjp(short_conv, proj_conv, conv_weights)
    rates, rates_pull = jax.vjp(
        rate_terms, proj_rates[:, :heads], proj_rates[:, heads:], a_log.astype(f32),
        dt_bias.astype(f32),
    )
    mixed, states, inverses = mixer_forward(
        conv_all, proj_gate, rates, gain_row, heads, key_dim, value_dim
    )
    row_values = tokens.astype(f32)
    scale_one, unit_one = norm_forward(row_values)
    normed_two, middle = turn(
        times_transpose(mixed, out_full).astype(bf16), tokens, gain_two, 2
    )
    gates_full, down_full = ffn_full[:, : 2 * ff], ffn_full[:, 2 * ff :]
    grad_hidden = jnp.dot(cot_full, down_full, preferred_element_type=f32)
    ups = jnp.dot(normed_two, gates_full, preferred_element_type=f32)
    up_gate, up_lin = ups[:, :ff], ups[:, ff:]
    gate_sigmoid = jax.nn.sigmoid(up_gate)
    hidden = (up_gate * gate_sigmoid * up_lin).astype(bf16)
    grad_gate = (
        grad_hidden * up_lin * gate_sigmoid * (1.0 + up_gate * (1.0 - gate_sigmoid))
    ).astype(bf16)
    grad_lin = (grad_hidden * up_gate * gate_sigmoid).astype(bf16)
    grad_ups = jnp.concatenate([grad_gate, grad_lin], axis=1)
    ffn_grads = jnp.concatenate(
        [
            weight_grad(normed_two, grad_ups).astype(bf16),
            weight_grad(cot_full, hidden).astype(bf16),
        ],
        axis=1,
    )
    grad_normed_part_two = times_transpose(grad_ups, gates_full).astype(bf16)
    grad_normed_part_two, ffn_grads = lax.optimization_barrier((grad_normed_part_two, ffn_grads))
    ffn_sums = lax.psum_scatter(ffn_grads, "dp", scatter_dimension=0, tiled=True)
    mid_full, grad_middle, grad_gain_two = turn(
        grad_normed_part_two, cotangent, gain_two, 3, middle
    )
    ranks = lax.axis_size("tensor")
    out_grads = weight_grad(mid_full, mixed).astype(bf16)
    result_part = times_transpose(hidden, down_full).astype(bf16)

    grad_mixed = jnp.dot(mid_full, out_full, preferred_element_type=f32)
    grad_conv_all, grad_pgate, grad_rates, grad_gain_row = mixer_backward(
        conv_all, proj_gate, rates, gain_row, states, inverses, grad_mixed,
        heads, key_dim, value_dim,
    )
    grad_pconv, grad_conv_w = conv_pull(grad_conv_all)
    grad_beta, grad_alpha, grad_rate_part, grad_bias_part = rates_pull(grad_rates)
    grad_proj = jnp.concatenate([grad_pconv.astype(bf16), grad_pgate.astype(bf16)], axis=1)
    grad_rate_proj = jnp.concatenate([grad_beta, grad_alpha], axis=1).astype(bf16)
    grad_normed_part = times_transpose(grad_proj, in_full) + jnp.dot(
        grad_rate_proj, rate_weights, preferred_element_type=f32
    )
    grad_gain_one = jnp.sum(grad_normed_part * unit_full, axis=0)
    grad_lines = jnp.concatenate(
        [grad_gain_one[None], grad_gain_two, weight_grad(grad_rate_proj, normed_one)], axis=0
    )
    edges = [0, qk_width, 2 * qk_width, conv_width]
    grad_small = small_block(
        [split_taps(grad_conv_w[:, edges[i] : edges[i + 1]], heads, dp) for i in range(3)]
        + [split_taps(grad_gain_row, heads, dp)],
        jnp.swapaxes(grad_lines.reshape(2 + 2 * heads, dp, shard_rows), 0, 1),
        f32,
    )
    rate_line = jnp.concatenate([grad_rate_part, grad_bias_part])
    rate_tile = jnp.pad(rate_line[None], ((0, 7), (0, LANES - 2 * heads)))
    in_grads = weight_grad(normed_one, grad_proj).astype(bf16)
    sums, swapped, rate_tiles, small_lines = reduce_all(
        [
            in_grads.reshape(dp, shard_rows, in_width),
            out_grads.reshape(dp, shard_rows, v_width),
            grad_small,
        ],
        [
            grad_normed_part.astype(bf16).reshape(ranks, -1, model),
            result_part.reshape(ranks, -1, model),
        ],
        rate_tile,
        7,
    )
    in_sums, out_sums, small_sums = sums
    grad_normed_one = jnp.sum(swapped[0].astype(f32), axis=0)
    result = (middle + jnp.sum(swapped[1].astype(f32), axis=0)).astype(bf16)
    grad_rows = grad_middle + norm_backward(grad_normed_one, unit_one, scale_one, gain_one)
    rate_sums = jnp.sum(rate_tiles, axis=0)[0]
    gain_sums = jnp.sum(small_lines[:, tap_lines : tap_lines + 2, :shard_rows], axis=0)
    ffn_sums = ffn_sums.astype(f32)

    def taps_out(index, lines):
        block = small_sums[:lines, lefts[index] : lefts[index] + lanes[index]]
        return jnp.transpose(block.reshape(heads, -1, lanes[index]), (2, 0, 1))

    def lines_out(first):
        return small_sums[tap_lines + first : tap_lines + first + heads, :shard_rows].T

    return (
        result,
        grad_rows,
        gain_sums[0],
        in_sums[:, :qk_width],
        in_sums[:, qk_width : 2 * qk_width],
        in_sums[:, 2 * qk_width : conv_width],
        in_sums[:, conv_width:],
        out_sums,
        lines_out(2),
        lines_out(2 + heads),
        taps_out(0, tap_lines),
        taps_out(1, tap_lines),
        taps_out(2, tap_lines),
        rate_sums[:heads],
        rate_sums[heads : 2 * heads],
        taps_out(3, heads)[:, :, 0],
        gain_sums[1],
        ffn_sums[:, :hidden_width],
        ffn_sums[:, ff : ff + hidden_width],
        ffn_sums[:, 2 * ff : 2 * ff + hidden_width],
    )


def solution(mesh):
    placed = (
        P(("dp", "tensor"), None),
        P(("dp", "tensor"), None),
        P("dp"),
        P("dp", "tensor"),
        P("dp", "tensor"),
        P("dp", "tensor"),
        P("dp", "tensor"),
        P("dp", "tensor"),
        P("dp", "tensor"),
        P("dp", "tensor"),
        P("dp", "tensor", None),
        P("dp", "tensor", None),
        P("dp", "tensor", None),
        P("tensor"),
        P("tensor"),
        P("dp", "tensor"),
        P("dp"),
        P("dp", "tensor"),
        P("dp", "tensor"),
        P("dp", "tensor"),
    )
    return jax.shard_map(
        on_device,
        mesh=mesh,
        in_specs=placed,
        out_specs=(
            P(("dp", "tensor"), None),
            P(("dp", "tensor"), None),
            P("dp"),
            P("dp", "tensor"),
            P("dp", "tensor"),
            P("dp", "tensor"),
            P("dp", "tensor"),
            P("dp", "tensor"),
            P("dp", "tensor"),
            P("dp", "tensor"),
            P("dp", "tensor", None),
            P("dp", "tensor", None),
            P("dp", "tensor", None),
            P("tensor"),
            P("tensor"),
            P("dp", "tensor"),
            P("dp"),
            P("dp", "tensor"),
            P("dp", "tensor"),
            P("dp", "tensor"),
        ),
        check_vma=False,
    )
```

```python
import jax
import jax.numpy as jnp
from jax import lax
from jax.experimental import pallas as pl
from jax.experimental.pallas import tpu as pltpu
from jax.sharding import PartitionSpec as P

epsilon = 1e-06
CHUNK = 128
LANES = 128
contract_rows = (((0,), (0,)), ((), ()))
contract_cols = (((1,), (1,)), ((), ()))
contract_plain = (((1,), (0,)), ((), ()))
highest = lax.Precision.HIGHEST


def norm_forward(row_values):
    row_scale = lax.rsqrt(jnp.mean(row_values * row_values, axis=-1, keepdims=True) + epsilon)
    return (row_scale, row_values * row_scale)


def norm_backward(grad_normed, unit_values, row_scale, gain_values):
    grad_unit = grad_normed * gain_values
    return row_scale * (
        grad_unit - unit_values * jnp.mean(grad_unit * unit_values, axis=-1, keepdims=True)
    )


def weight_grad(left_in, right_in):
    return lax.dot_general(left_in, right_in, contract_rows, preferred_element_type=jnp.float32)


def times_transpose(left_in, right_in):
    return lax.dot_general(left_in, right_in, contract_cols, preferred_element_type=jnp.float32)


def fine_dot(left_in, right_in, dims=contract_plain):
    return lax.dot_general(
        left_in, right_in, dims, precision=lax.Precision.HIGH, preferred_element_type=jnp.float32
    )


def exact_dot(left_in, right_in, dims=contract_plain):
    return fine_dot(left_in, right_in, dims)


def silu(values):
    return values * lax.logistic(values)


def unit_length(values):
    return values * lax.rsqrt(jnp.sum(values * values, axis=-1, keepdims=True) + epsilon)


def triangle_masks(size):
    row = lax.broadcasted_iota(jnp.int32, (size, size), 0)
    col = lax.broadcasted_iota(jnp.int32, (size, size), 1)
    return row, col


def unit_lower_inverses(lowers):
    size = lowers[0].shape[0]
    row, col = triangle_masks(size)
    eye = jnp.where(row == col, 1.0, 0.0)
    inverses = [eye for _ in lowers]
    bit = 0
    while (1 << bit) < size:
        joined = ((row >> (bit + 1)) == (col >> (bit + 1))) & ((row >> bit) != (col >> bit))
        parts = [jnp.where(joined, lower, 0.0) for lower in lowers]
        if bit == 0:
            inverses = [eye - part for part in parts]
        else:
            inner = [fine_dot(part, inverse) for part, inverse in zip(parts, inverses)]
            steps = [fine_dot(inverse, step) for inverse, step in zip(inverses, inner)]
            inverses = [inverse - step for inverse, step in zip(inverses, steps)]
        bit += 1
    return inverses


@jax.custom_vjp
def known_inverse(lower, inverse):
    return inverse


def known_inverse_fwd(lower, inverse):
    return inverse, inverse


def known_inverse_bwd(inverse, grad):
    turned = inverse.T
    return -fine_dot(fine_dot(turned, grad), turned), jnp.zeros_like(inverse)


known_inverse.defvjp(known_inverse_fwd, known_inverse_bwd)


def each(call, *lists):
    return [call(*items) for items in zip(*lists)]


def mixer_chunk(conv_q, conv_k, conv_v, proj_gate, beta, gate, gain, state, inverter):
    size, key_dim = conv_q[0].shape
    row, col = triangle_masks(size)
    strict = row > col
    lower = row >= col
    query = each(lambda v: unit_length(silu(v)) * key_dim ** (-0.5), conv_q)
    key = each(lambda v: unit_length(silu(v)), conv_k)
    value = each(silu, conv_v)
    wide = each(lambda g: jnp.broadcast_to(g, (size, size)), gate)
    decay_col = each(
        lambda w: jnp.sum(jnp.where(lower, w.T, 0.0), axis=1, keepdims=True), wide
    )
    decay_row = each(
        lambda w: jnp.sum(jnp.where(row <= col, w, 0.0), axis=0, keepdims=True), wide
    )
    decay_end = each(lambda g: jnp.sum(g, axis=0, keepdims=True), gate)
    differ = each(lambda c, r: jnp.where(strict, c - r, 0.0), decay_col, decay_row)
    decay = each(lambda d: jnp.where(lower, jnp.exp(d), 0.0), differ)
    grams = each(lambda k: exact_dot(k, k, contract_cols), key)
    system = each(lambda g, d, b: jnp.where(strict, g * d * b, 0.0), grams, decay, beta)
    inverse = inverter(system)
    grown = each(jnp.exp, decay_col)
    kept = each(lambda k, b, g, s: exact_dot(k * (b * g), s), key, beta, grown, state)
    fresh = each(lambda i, v, b, k: exact_dot(i, v * b - k), inverse, value, beta, kept)
    scores = each(lambda q, k, d: exact_dot(q, k, contract_cols) * d, query, key, decay)
    carried = each(lambda q, g, s: exact_dot(q * g, s), query, grown, state)
    mixed = each(lambda c, s, f: c + exact_dot(s, f), carried, scores, fresh)
    added = each(
        lambda k, e, c, f: exact_dot(k * jnp.exp(e - c), f, contract_rows),
        key, decay_end, decay_col, fresh,
    )
    new_state = each(lambda e, s, a: jnp.exp(e) * s + a, decay_end, state, added)
    gated = each(
        lambda m, g, p: m
        * lax.rsqrt(jnp.mean(m * m, axis=-1, keepdims=True) + epsilon)
        * g
        * silu(p),
        mixed, gain, proj_gate,
    )
    return gated, new_state, inverse


def head_slices(head, heads, key_dim, value_dim):
    q_at = head * key_dim
    k_at = (heads + head) * key_dim
    v_at = 2 * heads * key_dim + head * value_dim
    return (
        slice(q_at, q_at + key_dim),
        slice(k_at, k_at + key_dim),
        slice(v_at, v_at + value_dim),
        slice(head * value_dim, (head + 1) * value_dim),
    )


def head_inputs(heads, key_dim, value_dim, conv_ref, pgate_ref, rates_ref, gain_ref):
    at = [head_slices(head, heads, key_dim, value_dim) for head in range(heads)]
    return at, (
        [conv_ref[:, spots[0]] for spots in at],
        [conv_ref[:, spots[1]] for spots in at],
        [conv_ref[:, spots[2]] for spots in at],
        [pgate_ref[:, spots[3]] for spots in at],
        [rates_ref[:, head : head + 1] for head in range(heads)],
        [rates_ref[:, heads + head : heads + head + 1] for head in range(heads)],
        [gain_ref[:, spots[3]] for spots in at],
    )


def mixer_forward_kernel(
    heads, key_dim, value_dim, conv_ref, pgate_ref, rates_ref, gain_ref,
    gated_ref, states_ref, inverses_ref, state_ref,
):
    @pl.when(pl.program_id(0) == 0)
    def _():
        state_ref[...] = jnp.zeros_like(state_ref)

    at, operands = head_inputs(
        heads, key_dim, value_dim, conv_ref, pgate_ref, rates_ref, gain_ref
    )
    state = [state_ref[head] for head in range(heads)]
    gated, new_state, inverse = mixer_chunk(*operands, state, unit_lower_inverses)
    for head in range(heads):
        gated_ref[:, at[head][3]] = gated[head].astype(gated_ref.dtype)
        states_ref[0, head] = state[head]
        inverses_ref[0, head] = inverse[head]
        state_ref[head] = new_state[head]


def mixer_backward_kernel(
    heads, key_dim, value_dim, conv_ref, pgate_ref, rates_ref, gain_ref, states_ref,
    inverses_ref, grad_ref, gconv_ref, gpgate_ref, grates_ref, ggain_ref, gstate_ref,
):
    @pl.when(pl.program_id(0) == 0)
    def _():
        gstate_ref[...] = jnp.zeros_like(gstate_ref)
        ggain_ref[...] = jnp.zeros_like(ggain_ref)

    lane = lax.broadcasted_iota(jnp.int32, grates_ref.shape, 1)
    rates_grad = jnp.zeros(grates_ref.shape, jnp.float32)
    at, operands = head_inputs(
        heads, key_dim, value_dim, conv_ref, pgate_ref, rates_ref, gain_ref
    )
    inverses = [inverses_ref[0, head] for head in range(heads)]

    def run(*operands):
        gated, new_state, _ = mixer_chunk(
            *operands, lambda systems: each(known_inverse, systems, inverses)
        )
        return gated, new_state

    _, pull = jax.vjp(run, *operands, [states_ref[0, head] for head in range(heads)])
    pulled = pull(
        (
            [grad_ref[:, spots[3]] for spots in at],
            [gstate_ref[head] for head in range(heads)],
        )
    )
    for head in range(heads):
        at_q, at_k, at_v, at_g = at[head]
        gconv_ref[:, at_q] = pulled[0][head]
        gconv_ref[:, at_k] = pulled[1][head]
        gconv_ref[:, at_v] = pulled[2][head]
        gpgate_ref[:, at_g] = pulled[3][head]
        rates_grad = jnp.where(lane == head, pulled[4][head], rates_grad)
        rates_grad = jnp.where(lane == heads + head, pulled[5][head], rates_grad)
        ggain_ref[:, at_g] += pulled[6][head]
        gstate_ref[head] = pulled[7][head]
    grates_ref[...] = rates_grad


def row_block(width, order):
    return pl.BlockSpec((CHUNK, width), lambda step: (order(step), 0))


def mixer_forward(conv_all, proj_gate, rates, gain_row, heads, key_dim, value_dim):
    rows, conv_width = conv_all.shape
    steps = rows // CHUNK
    forward = lambda step: step
    width = heads * value_dim
    return pl.pallas_call(
        lambda *refs: mixer_forward_kernel(heads, key_dim, value_dim, *refs),
        name="mixer_forward",
        grid=(steps,),
        in_specs=[
            row_block(conv_width, forward),
            row_block(width, forward),
            row_block(rates.shape[1], forward),
            pl.BlockSpec((1, width), lambda step: (0, 0)),
        ],
        out_specs=[
            row_block(width, forward),
            pl.BlockSpec((1, heads, key_dim, value_dim), lambda step: (step, 0, 0, 0)),
            pl.BlockSpec((1, heads, CHUNK, CHUNK), lambda step: (step, 0, 0, 0)),
        ],
        out_shape=[
            jax.ShapeDtypeStruct((rows, width), jnp.bfloat16),
            jax.ShapeDtypeStruct((steps, heads, key_dim, value_dim), jnp.float32),
            jax.ShapeDtypeStruct((steps, heads, CHUNK, CHUNK), jnp.float32),
        ],
        scratch_shapes=[pltpu.VMEM((heads, key_dim, value_dim), jnp.float32)],
        cost_estimate=pl.CostEstimate(
            flops=30_000_000_000, bytes_accessed=8_000_000, transcendentals=1_000_000
        ),
    )(conv_all, proj_gate, rates, gain_row)


def mixer_backward(
    conv_all, proj_gate, rates, gain_row, states, inverses, grad_gated, heads, key_dim, value_dim
):
    rows, conv_width = conv_all.shape
    steps = rows // CHUNK
    back = lambda step: steps - 1 - step
    width = heads * value_dim
    return pl.pallas_call(
        lambda *refs: mixer_backward_kernel(heads, key_dim, value_dim, *refs),
        name="mixer_backward",
        grid=(steps,),
        in_specs=[
            row_block(conv_width, back),
            row_block(width, back),
            row_block(rates.shape[1], back),
            pl.BlockSpec((1, width), lambda step: (0, 0)),
            pl.BlockSpec((1, heads, key_dim, value_dim), lambda step: (back(step), 0, 0, 0)),
            pl.BlockSpec((1, heads, CHUNK, CHUNK), lambda step: (back(step), 0, 0, 0)),
            row_block(width, back),
        ],
        out_specs=[
            row_block(conv_width, back),
            row_block(width, back),
            row_block(rates.shape[1], back),
            pl.BlockSpec((1, width), lambda step: (0, 0)),
        ],
        out_shape=[
            jax.ShapeDtypeStruct((rows, conv_width), jnp.float32),
            jax.ShapeDtypeStruct((rows, width), jnp.float32),
            jax.ShapeDtypeStruct(rates.shape, jnp.float32),
            jax.ShapeDtypeStruct((1, width), jnp.float32),
        ],
        scratch_shapes=[pltpu.VMEM((heads, key_dim, value_dim), jnp.float32)],
        cost_estimate=pl.CostEstimate(
            flops=30_000_000_000, bytes_accessed=12_000_000, transcendentals=2_000_000
        ),
    )(conv_all, proj_gate, rates, gain_row, states, inverses, grad_gated)


def ring_position(index, size):
    if size % 2:
        return index
    side, line = index % 2, index // 2
    return line + side * (size - 1 - 2 * line)


def ring_index(position, size):
    if size % 2:
        return position
    side = position // (size // 2)
    line = position + side * (size - 1 - 2 * position)
    return line * 2 + side


def greet(peers):
    barrier = pltpu.get_barrier_semaphore()
    for target in peers:
        pl.semaphore_signal(
            barrier, inc=1, device_id=target, device_id_type=pl.DeviceIdType.MESH
        )
    pl.semaphore_wait(barrier, len(peers))


def send(source, place, sent, landed, target):
    copy = pltpu.make_async_remote_copy(
        src_ref=source,
        dst_ref=place,
        send_sem=sent,
        recv_sem=landed,
        device_id=target,
        device_id_type=pl.DeviceIdType.MESH,
    )
    copy.start()
    return copy


def others(axis):
    ranks = lax.axis_size(axis)
    mine = lax.axis_index(axis)
    return [lax.rem(mine + step, ranks) for step in range(1, ranks)]


def ring_ends(dp):
    at = ring_position(lax.axis_index("dp"), dp)
    after = ring_index((at + 1) % dp, dp)
    before = ring_index((at + dp - 1) % dp, dp)
    return at, after, before


def gather_kernel(dp, ranks, widths, count, *refs):
    parts = len(widths) + 1
    shards, rows = refs[:parts], refs[parts : parts + count]
    full_ref, last_ref, small_ref = refs[parts + count : parts + count + 3]
    gots = refs[parts + count + 3 : parts + 2 * count + 3]
    own_sems, ring_sent, ring_got, row_sent, row_got = refs[parts + 2 * count + 3 :]
    me, mine = lax.axis_index("dp"), lax.axis_index("tensor")
    at, after, before = ring_ends(dp)
    peers = others("tensor")
    ends = [{"dp": after}, {"dp": before}]
    greet(ends + [{"tensor": peer} for peer in peers])
    lefts = [sum(widths[:part]) for part in range(parts)]
    hops = [[(dp - 1 + (part + way) % 2) // 2 for part in range(parts)] for way in range(2)]

    def place(owner, part):
        if part == parts - 1:
            return small_ref.at[owner]
        if part == parts - 2:
            return last_ref.at[owner]
        return full_ref.at[owner, :, pl.ds(lefts[part], widths[part])]

    flying = {}

    def hop(way, step, part):
        owner = ring_index((at + (dp - step if way == 0 else step)) % dp, dp)
        spot = place(owner, part)
        flying[way, step, part] = send(
            shards[part] if step == 0 else spot,
            spot,
            ring_sent.at[way, step, part],
            ring_got.at[way, step, part],
            ends[way],
        )

    for part in range(parts):
        for way in range(2):
            if hops[way][part] > 0:
                hop(way, 0, part)
    swaps = []
    for step, peer in enumerate(peers):
        for index in range(count):
            swaps.append(
                send(
                    rows[index],
                    gots[index].at[mine],
                    row_sent.at[step, index],
                    row_got.at[step, index],
                    {"tensor": peer},
                )
            )
    local = []
    for part in range(parts):
        local.append(pltpu.make_async_copy(shards[part], place(me, part), own_sems.at[part]))
    for index in range(count):
        local.append(
            pltpu.make_async_copy(rows[index], gots[index].at[mine], own_sems.at[parts + index])
        )
    for copy in local:
        copy.start()
    for step in range(1, max(max(line) for line in hops) + 1):
        for part in range(parts):
            for way in range(2):
                if hops[way][part] >= step:
                    flying[way, step - 1, part].wait_recv()
                    if hops[way][part] > step:
                        hop(way, step, part)
    for copy in local + swaps:
        copy.wait()
    for copy in flying.values():
        copy.wait_send()


def gather_all(shards, small, rows, number):
    dp, ranks = lax.axis_size("dp"), lax.axis_size("tensor")
    widths = [shard.shape[1] for shard in shards]
    parts, count = len(shards) + 1, len(rows)
    anywhere = pl.BlockSpec(memory_space=pl.ANY)
    vmem = pl.BlockSpec(memory_space=pltpu.VMEM)
    sem = pltpu.SemaphoreType.DMA
    got = pl.pallas_call(
        lambda *refs: gather_kernel(dp, ranks, widths, count, *refs),
        name="gather_all",
        in_specs=[anywhere] * (parts + count),
        out_specs=[vmem] * (3 + count),
        out_shape=[
            jax.ShapeDtypeStruct((dp, shards[0].shape[0], sum(widths[:-1])), shards[0].dtype),
            jax.ShapeDtypeStruct((dp,) + shards[-1].shape, shards[-1].dtype),
            jax.ShapeDtypeStruct((dp,) + small.shape, small.dtype),
        ]
        + [jax.ShapeDtypeStruct((ranks,) + block.shape, block.dtype) for block in rows],
        scratch_shapes=[
            sem((parts + count,)),
            sem((2, max(1, dp // 2), parts)),
            sem((2, max(1, dp // 2), parts)),
            sem((ranks - 1, count)),
            sem((ranks - 1, count)),
        ],
        compiler_params=pltpu.CompilerParams(collective_id=number, has_side_effects=True),
        cost_estimate=pl.CostEstimate(
            flops=30_000_000_000, bytes_accessed=16_000_000, transcendentals=0
        ),
    )(*shards, small, *rows)
    full, last, *blocks = [block.reshape(-1, block.shape[-1]) for block in got[:2] + got[3:]]
    return full, last, got[2], blocks


def reduce_kernel(dp, ranks, lines, count, cuts, *refs):
    arrays = count[0]
    grads, swaps_in, tile_ref = refs[:arrays], refs[arrays : arrays + count[1]], refs[arrays + count[1]]
    refs = refs[arrays + count[1] + 1 :]
    sums = []
    for cut in cuts:
        sums.append(refs[: len(cut)])
        refs = refs[len(cut) :]
    swaps_out = refs[: count[1]]
    tiles_ref, lines_ref = refs[count[1] : count[1] + 2]
    refs = refs[count[1] + 2 :]
    landed, totals = refs[:arrays], refs[arrays : 2 * arrays]
    ring_sent, ring_got, row_sent, row_got, tile_sent, tile_got, line_sent, line_got = refs[
        2 * arrays :
    ]
    me, mine = lax.axis_index("dp"), lax.axis_index("tensor")
    at, after, before = ring_ends(dp)
    peers, mates = others("tensor"), others("dp")
    ends = [{"dp": after}, {"dp": before}]
    greet([{"dp": mate} for mate in mates] + [{"tensor": peer} for peer in peers])
    last = dp - 2

    def owner(way, step):
        return ring_index((at + (2 * dp - 1 - step if way == 0 else 1 + step)) % dp, dp)

    flying = {}

    def hop(line, step):
        array, top, rows, way = lines[line]
        span = pl.ds(top, rows)
        source = grads[array].at[owner(way, 0), span] if step == 0 else totals[array].at[step - 1, span]
        flying[line, step] = send(
            source,
            landed[array].at[step, span],
            ring_sent.at[line, step],
            ring_got.at[line, step],
            ends[way],
        )

    for line in range(len(lines)):
        hop(line, 0)
    copies = []
    for step, mate in enumerate(mates):
        copies.append(
            send(tile_ref, tiles_ref.at[me], tile_sent.at[step], tile_got.at[step], {"dp": mate})
        )
    for index in range(count[1]):
        for step, peer in enumerate(peers):
            copies.append(
                send(
                    swaps_in[index].at[peer],
                    swaps_out[index].at[mine],
                    row_sent.at[step, index],
                    row_got.at[step, index],
                    {"tensor": peer},
                )
            )
    tiles_ref[me] = tile_ref[...]
    for index in range(count[1]):
        swaps_out[index][mine] = swaps_in[index][mine]
    for step in range(dp - 1):
        for line, (array, top, rows, way) in enumerate(lines):
            flying[line, step].wait_recv()
            span = pl.ds(top, rows)
            own = me if step == last else owner(way, step + 1)
            total = landed[array][step, span].astype(jnp.float32) + grads[array][
                own, span
            ].astype(jnp.float32)
            if step == last:
                for (left, width), sum_ref in zip(cuts[array], sums[array]):
                    sum_ref[span] = total[:, left : left + width]
            else:
                totals[array][step, span] = total.astype(totals[array].dtype)
                hop(line, step + 1)
    small = sums[arrays - 1][0]
    for step, peer in enumerate(peers):
        copies.append(
            send(small, lines_ref.at[mine], line_sent.at[step], line_got.at[step], {"tensor": peer})
        )
    lines_ref[mine] = small[...]
    for copy in copies:
        copy.wait()
    for copy in flying.values():
        copy.wait_send()


def reduce_all(grads, swaps, tile, number, splits):
    dp, ranks = lax.axis_size("dp"), lax.axis_size("tensor")
    vmem = pl.BlockSpec(memory_space=pltpu.VMEM)
    sem = pltpu.SemaphoreType.DMA
    lines = []
    for array, grad in enumerate(grads):
        rows = grad.shape[1]
        pieces = 4 if rows * grad.shape[2] > 100_000 and rows % 64 == 0 else 2
        for piece in range(pieces):
            lines.append((array, piece * rows // pieces, rows // pieces, piece % 2))
    lines = lines[-2:] + lines[:-2]
    count = (len(grads), len(swaps))
    cuts = []
    for widths in splits:
        cuts.append([(sum(widths[:index]), width) for index, width in enumerate(widths)])
    pieces = [
        jax.ShapeDtypeStruct((grad.shape[1], width), jnp.float32)
        for grad, widths in zip(grads, splits)
        for width in widths
    ]
    inputs = list(grads) + list(swaps) + [tile]
    small = grads[-1].shape[1:]
    results = pl.pallas_call(
        lambda *refs: reduce_kernel(dp, ranks, lines, count, cuts, *refs),
        name="reduce_all",
        in_specs=[vmem] * len(inputs),
        out_specs=[vmem] * (len(pieces) + len(swaps) + 2),
        out_shape=pieces
        + [jax.ShapeDtypeStruct(block.shape, block.dtype) for block in swaps]
        + [
            jax.ShapeDtypeStruct((dp,) + tile.shape, tile.dtype),
            jax.ShapeDtypeStruct((ranks,) + small, jnp.float32),
        ],
        scratch_shapes=[pltpu.VMEM((dp - 1,) + grad.shape[1:], grad.dtype) for grad in grads]
        + [pltpu.VMEM((dp - 1,) + grad.shape[1:], grad.dtype) for grad in grads]
        + [
            sem((len(lines), dp - 1)),
            sem((len(lines), dp - 1)),
            sem((ranks - 1, len(swaps))),
            sem((ranks - 1, len(swaps))),
            sem((dp - 1,)),
            sem((dp - 1,)),
            sem((ranks - 1,)),
            sem((ranks - 1,)),
        ],
        compiler_params=pltpu.CompilerParams(collective_id=number, has_side_effects=True),
        cost_estimate=pl.CostEstimate(
            flops=30_000_000_000, bytes_accessed=16_000_000, transcendentals=0
        ),
    )(*inputs)
    arrays = len(pieces)
    return results[:arrays], results[arrays : arrays + len(swaps)], results[-2], results[-1]


def forward_finish(summed, tokens_ref, gain_ref, middle_ref, span):
    middle = tokens_ref[span].astype(jnp.float32) + summed
    middle_ref[span] = middle
    _, unit = norm_forward(middle)
    return unit * gain_ref[...]


def backward_finish(summed, cotangent_ref, gain_ref, middle_ref, grad_ref, gain_grad_ref, span):
    scale, unit = norm_forward(middle_ref[span])
    gain_grad_ref[...] += jnp.sum(summed * unit, axis=0, keepdims=True)
    grad = cotangent_ref[span].astype(jnp.float32) + norm_backward(
        summed, unit, scale, gain_ref[...]
    )
    grad_ref[span] = grad
    return grad


def turn_kernel(ranks, chunks, backward, *refs):
    if backward:
        part_ref, rows_ref, gain_ref, middle_ref, got_ref, grad_ref, gain_grad_ref = refs[:7]
        scratch = refs[7:]
        gain_grad_ref[...] = jnp.zeros_like(gain_grad_ref)
    else:
        part_ref, rows_ref, gain_ref, got_ref, middle_ref = refs[:5]
        scratch = refs[5:]
    pair_buf, sum_buf, far_buf, pair_s, pair_r, far_s, far_r, out_s, out_r, on_s, on_r = scratch
    mine = lax.axis_index("tensor")
    side, group = mine % 2, mine // 2
    groups = ranks // 2
    partner = group * 2 + 1 - side
    away = [(group + step) % groups for step in range(1, groups)]
    mates = [{"tensor": other * 2 + side} for other in away]
    near = {"tensor": partner}
    greet([near] + mates)
    rows = part_ref.shape[1] // chunks
    flying = []
    spans = [pl.ds(chunk * rows, rows) for chunk in range(chunks)]

    def go(*operands):
        copy = send(*operands)
        flying.append(copy)
        return copy

    pairs, fars, outs, ons, backs = {}, {}, {}, {}, {}
    order = away + [group]
    for chunk, span in enumerate(spans):
        for step, other in enumerate(order):
            pairs[step, chunk] = go(
                part_ref.at[other * 2 + 1 - side, span],
                pair_buf.at[step, span],
                pair_s.at[step, chunk],
                pair_r.at[step, chunk],
                near,
            )
    for chunk, span in enumerate(spans):
        for step, other in enumerate(away):
            pairs[step, chunk].wait_recv()
            total = part_ref[other * 2 + side, span].astype(jnp.float32) + pair_buf[
                step, span
            ].astype(jnp.float32)
            sum_buf[step, span] = total.astype(sum_buf.dtype)
            fars[step, chunk] = go(
                sum_buf.at[step, span],
                far_buf.at[step, span],
                far_s.at[step, chunk],
                far_r.at[step, chunk],
                mates[step],
            )
    for chunk, span in enumerate(spans):
        pairs[groups - 1, chunk].wait_recv()
        summed = part_ref[mine, span].astype(jnp.float32) + pair_buf[groups - 1, span].astype(
            jnp.float32
        )
        for step in range(groups - 1):
            fars[step, chunk].wait_recv()
            summed = summed + far_buf[step, span].astype(jnp.float32)
        if backward:
            done = backward_finish(
                summed, rows_ref, gain_ref, middle_ref, grad_ref, gain_grad_ref, span
            )
        else:
            done = forward_finish(summed, rows_ref, gain_ref, middle_ref, span)
        got_ref[mine, span] = done.astype(got_ref.dtype)
        place = got_ref.at[mine, span]
        for step in range(groups - 1):
            outs[step, chunk] = go(
                place, place, out_s.at[step, chunk], out_r.at[step, chunk], mates[step]
            )
        ons[groups - 1, chunk] = go(
            place, place, on_s.at[groups - 1, chunk], on_r.at[groups - 1, chunk], near
        )
    for chunk, span in enumerate(spans):
        for step in range(groups - 1):
            outs[step, chunk].wait_recv()
            source = ((group + groups - 1 - step) % groups) * 2 + side
            place = got_ref.at[source, span]
            ons[step, chunk] = go(
                place, place, on_s.at[step, chunk], on_r.at[step, chunk], near
            )
    for chunk in range(chunks):
        for step in range(groups):
            ons[step, chunk].wait_recv()
    for copy in flying:
        copy.wait_send()


def turn(part, own_rows, gain, number, middle=None, chunks=4):
    ranks = lax.axis_size("tensor")
    rows, model = own_rows.shape
    chunks = chunks if rows % (16 * chunks) == 0 else 1
    groups = ranks // 2
    backward = middle is not None
    vmem = pl.BlockSpec(memory_space=pltpu.VMEM)
    sem = pltpu.SemaphoreType.DMA
    out_shape = [
        jax.ShapeDtypeStruct((ranks, rows, model), jnp.bfloat16),
        jax.ShapeDtypeStruct((rows, model), jnp.float32),
    ]
    inputs = [part.reshape(ranks, rows, model), own_rows, gain]
    if backward:
        out_shape.append(jax.ShapeDtypeStruct((1, model), jnp.float32))
        inputs.append(middle)
    results = pl.pallas_call(
        lambda *refs: turn_kernel(ranks, chunks, backward, *refs),
        name="turn_backward" if backward else "turn_forward",
        in_specs=[vmem] * len(inputs),
        out_specs=[vmem] * len(out_shape),
        out_shape=out_shape,
        scratch_shapes=[
            pltpu.VMEM((groups, rows, model), jnp.bfloat16),
            pltpu.VMEM((max(1, groups - 1), rows, model), jnp.bfloat16),
            pltpu.VMEM((max(1, groups - 1), rows, model), jnp.bfloat16),
        ]
        + [sem((groups, chunks))] * 8,
        compiler_params=pltpu.CompilerParams(collective_id=number, has_side_effects=True),
        cost_estimate=pl.CostEstimate(
            flops=10_000_000_000, bytes_accessed=4_000_000, transcendentals=0
        ),
    )(*inputs)
    return (results[0].reshape(-1, model),) + tuple(results[1:])


def short_conv(inputs, weights):
    tap_count = weights.shape[0]
    row_count = inputs.shape[0]
    padded = jnp.pad(inputs, ((tap_count - 1, 0), (0, 0)))
    result = jnp.zeros_like(inputs)
    for offset in range(tap_count):
        result = result + padded[offset : offset + row_count] * weights[offset]
    return result


def round_up(size, step):
    return -(-size // step) * step


def pad_columns(matrix_in, width):
    return jnp.pad(matrix_in, ((0, 0), (0, width - matrix_in.shape[1])))


def tap_rows(conv_weights):
    channels, heads, taps = conv_weights.shape
    return jnp.transpose(conv_weights, (1, 2, 0)).reshape(heads * taps, channels)


def joined_taps(rows, heads):
    shards, _, channels = rows.shape
    split = rows.reshape(shards, heads, -1, channels)
    taps = split.shape[2]
    return jnp.transpose(split, (2, 1, 0, 3)).reshape(taps, heads * shards * channels)


def split_taps(taps_in, heads, shards):
    taps, width = taps_in.shape
    split = taps_in.reshape(taps, heads, shards, width // (heads * shards))
    return jnp.transpose(split, (2, 1, 0, 3)).reshape(shards, heads * taps, -1)


def rate_terms(proj_beta, proj_alpha, log_rate, rate_bias):
    log_gates = -jnp.exp(log_rate) * jax.nn.softplus(proj_alpha + rate_bias)
    return jnp.concatenate([jax.nn.sigmoid(proj_beta), log_gates], axis=1)


def on_device(
    tokens, cotangent, norm1_gain, w_query, w_key, w_value, w_gate_out, w_out, w_beta, w_alpha,
    conv_query, conv_key, conv_value, a_log, dt_bias, head_gain, norm2_gain, w_up_gate, w_up,
    w_down,
):
    bf16, f32 = jnp.bfloat16, jnp.float32
    shard_rows, model = w_query.shape[0], tokens.shape[1]
    dp = model // shard_rows
    heads = a_log.shape[0]
    key_dim, value_dim = w_query.shape[1] // heads, w_value.shape[1] // heads
    taps = conv_query.shape[2]
    tap_lines = heads * taps
    qk_width, v_width = heads * key_dim, heads * value_dim
    conv_width = 2 * qk_width + v_width
    in_width = conv_width + v_width
    hidden_width = w_up.shape[1]
    ff = round_up(hidden_width, 256)

    packed = [tap_rows(conv_query), tap_rows(conv_key), tap_rows(conv_value), head_gain.T]
    lanes = [block.shape[1] for block in packed]
    lefts = [sum(lanes[:index]) for index in range(4)]
    line_rows = tap_lines + 2 + 2 * heads
    small_rows = round_up(line_rows, 16)
    small_width = round_up(max(sum(lanes), shard_rows), LANES)

    def small_block(groups, lines, kind):
        shards = groups[0].shape[0]
        group = jnp.concatenate(
            [jnp.pad(g, ((0, 0), (0, tap_lines - g.shape[1]), (0, 0))) for g in groups], axis=2
        )
        group = jnp.pad(group, ((0, 0), (0, 0), (0, small_width - sum(lanes))))
        lines = jnp.pad(lines, ((0, 0), (0, 0), (0, small_width - lines.shape[2])))
        rest = jnp.zeros((shards, small_rows - line_rows, small_width), kind)
        return jnp.concatenate([group.astype(kind), lines.astype(kind), rest], axis=1)

    small = small_block(
        [block[None] for block in packed],
        jnp.concatenate([norm1_gain[None], norm2_gain[None], w_beta.T, w_alpha.T], axis=0)[None],
        bf16,
    )[0]
    ffn_pack = jnp.concatenate([pad_columns(w, ff) for w in (w_up_gate, w_up, w_down)], axis=1)
    ffn_full = lax.all_gather(ffn_pack, "dp", axis=0, tiled=True)
    in_full, out_full, small_full, (tokens_got, cot_full) = gather_all(
        [w_query, w_key, w_value, w_gate_out, w_out], small, [tokens, cotangent], 1
    )
    small_all = small_full.astype(f32)

    def group_of(index, rows):
        return small_all[:, :rows, lefts[index] : lefts[index] + lanes[index]]

    def line_of(first, count):
        lines = small_all[:, tap_lines + first : tap_lines + first + count, :shard_rows]
        return jnp.swapaxes(lines, 0, 1).reshape(count, model)

    gain_one, gain_two = line_of(0, 1), line_of(1, 1)
    rate_weights = line_of(2, 2 * heads).astype(bf16)
    conv_weights = jnp.concatenate(
        [joined_taps(group_of(index, tap_lines), heads) for index in range(3)], axis=1
    )
    gain_row = joined_taps(group_of(3, heads), heads)

    tokens_full = tokens_got.astype(f32)
    _, unit_full = norm_forward(tokens_full)
    normed_one = (unit_full * gain_one).astype(bf16)
    projected = jnp.dot(normed_one, in_full, preferred_element_type=f32)
    proj_rates = times_transpose(normed_one, rate_weights)
    proj_conv = projected[:, :conv_width]
    proj_gate = projected[:, conv_width:]
    conv_all, conv_pull = jax.vjp(short_conv, proj_conv, conv_weights)
    rates, rates_pull = jax.vjp(
        rate_terms, proj_rates[:, :heads], proj_rates[:, heads:], a_log.astype(f32),
        dt_bias.astype(f32),
    )
    mixed, states, inverses = mixer_forward(
        conv_all, proj_gate, rates, gain_row, heads, key_dim, value_dim
    )
    row_values = tokens.astype(f32)
    scale_one, unit_one = norm_forward(row_values)
    normed_two, middle = turn(
        times_transpose(mixed, out_full).astype(bf16), tokens, gain_two, 2
    )
    gates_full, down_full = ffn_full[:, : 2 * ff], ffn_full[:, 2 * ff :]
    grad_hidden = jnp.dot(cot_full, down_full, preferred_element_type=f32)
    ups = jnp.dot(normed_two, gates_full, preferred_element_type=f32)
    up_gate, up_lin = ups[:, :ff], ups[:, ff:]
    gate_sigmoid = jax.nn.sigmoid(up_gate)
    hidden = (up_gate * gate_sigmoid * up_lin).astype(bf16)
    grad_gate = (
        grad_hidden * up_lin * gate_sigmoid * (1.0 + up_gate * (1.0 - gate_sigmoid))
    ).astype(bf16)
    grad_lin = (grad_hidden * up_gate * gate_sigmoid).astype(bf16)
    grad_ups = jnp.concatenate([grad_gate, grad_lin], axis=1)
    ffn_grads = jnp.concatenate(
        [
            weight_grad(normed_two, grad_ups).astype(bf16),
            weight_grad(cot_full, hidden).astype(bf16),
        ],
        axis=1,
    )
    grad_normed_part_two = times_transpose(grad_ups, gates_full).astype(bf16)
    grad_normed_part_two, ffn_grads = lax.optimization_barrier((grad_normed_part_two, ffn_grads))
    ffn_sums = lax.psum_scatter(ffn_grads, "dp", scatter_dimension=0, tiled=True)
    mid_full, grad_middle, grad_gain_two = turn(
        grad_normed_part_two, cotangent, gain_two, 3, middle
    )
    ranks = lax.axis_size("tensor")
    out_grads = weight_grad(mid_full, mixed).astype(bf16)
    result_part = times_transpose(hidden, down_full).astype(bf16)

    grad_mixed = jnp.dot(mid_full, out_full, preferred_element_type=f32)
    grad_conv_all, grad_pgate, grad_rates, grad_gain_row = mixer_backward(
        conv_all, proj_gate, rates, gain_row, states, inverses, grad_mixed,
        heads, key_dim, value_dim,
    )
    grad_pconv, grad_conv_w = conv_pull(grad_conv_all)
    grad_beta, grad_alpha, grad_rate_part, grad_bias_part = rates_pull(grad_rates)
    grad_proj = jnp.concatenate([grad_pconv.astype(bf16), grad_pgate.astype(bf16)], axis=1)
    grad_rate_proj = jnp.concatenate([grad_beta, grad_alpha], axis=1).astype(bf16)
    grad_normed_part = times_transpose(grad_proj, in_full) + jnp.dot(
        grad_rate_proj, rate_weights, preferred_element_type=f32
    )
    grad_gain_one = jnp.sum(grad_normed_part * unit_full, axis=0)
    grad_lines = jnp.concatenate(
        [grad_gain_one[None], grad_gain_two, weight_grad(grad_rate_proj, normed_one)], axis=0
    )
    edges = [0, qk_width, 2 * qk_width, conv_width]
    grad_small = small_block(
        [split_taps(grad_conv_w[:, edges[i] : edges[i + 1]], heads, dp) for i in range(3)]
        + [split_taps(grad_gain_row, heads, dp)],
        jnp.swapaxes(grad_lines.reshape(2 + 2 * heads, dp, shard_rows), 0, 1),
        f32,
    )
    rate_line = jnp.concatenate([grad_rate_part, grad_bias_part])
    rate_tile = jnp.pad(rate_line[None], ((0, 7), (0, LANES - 2 * heads)))
    in_grads = weight_grad(normed_one, grad_proj).astype(bf16)
    sums, swapped, rate_tiles, small_lines = reduce_all(
        [
            in_grads.reshape(dp, shard_rows, in_width),
            out_grads.reshape(dp, shard_rows, v_width),
            grad_small,
        ],
        [
            grad_normed_part.astype(bf16).reshape(ranks, -1, model),
            result_part.reshape(ranks, -1, model),
        ],
        rate_tile,
        7,
        [[qk_width, qk_width, v_width, v_width], [v_width], [small_width]],
    )
    query_sums, key_sums, value_sums, gate_sums, out_sums, small_sums = sums
    grad_normed_one = jnp.sum(swapped[0].astype(f32), axis=0)
    result = (middle + jnp.sum(swapped[1].astype(f32), axis=0)).astype(bf16)
    grad_rows = grad_middle + norm_backward(grad_normed_one, unit_one, scale_one, gain_one)
    rate_sums = jnp.sum(rate_tiles, axis=0)[0]
    gain_sums = jnp.sum(small_lines[:, tap_lines : tap_lines + 2, :shard_rows], axis=0)
    ffn_sums = ffn_sums.astype(f32)

    def taps_out(index, lines):
        block = small_sums[:lines, lefts[index] : lefts[index] + lanes[index]]
        return jnp.transpose(block.reshape(heads, -1, lanes[index]), (2, 0, 1))

    def lines_out(first):
        return small_sums[tap_lines + first : tap_lines + first + heads, :shard_rows].T

    return (
        result,
        grad_rows,
        gain_sums[0],
        query_sums,
        key_sums,
        value_sums,
        gate_sums,
        out_sums,
        lines_out(2),
        lines_out(2 + heads),
        taps_out(0, tap_lines),
        taps_out(1, tap_lines),
        taps_out(2, tap_lines),
        rate_sums[:heads],
        rate_sums[heads : 2 * heads],
        taps_out(3, heads)[:, :, 0],
        gain_sums[1],
        ffn_sums[:, :hidden_width],
        ffn_sums[:, ff : ff + hidden_width],
        ffn_sums[:, 2 * ff : 2 * ff + hidden_width],
    )


def solution(mesh):
    placed = (
        P(("dp", "tensor"), None),
        P(("dp", "tensor"), None),
        P("dp"),
        P("dp", "tensor"),
        P("dp", "tensor"),
        P("dp", "tensor"),
        P("dp", "tensor"),
        P("dp", "tensor"),
        P("dp", "tensor"),
        P("dp", "tensor"),
        P("dp", "tensor", None),
        P("dp", "tensor", None),
        P("dp", "tensor", None),
        P("tensor"),
        P("tensor"),
        P("dp", "tensor"),
        P("dp"),
        P("dp", "tensor"),
        P("dp", "tensor"),
        P("dp", "tensor"),
    )
    return jax.shard_map(
        on_device,
        mesh=mesh,
        in_specs=placed,
        out_specs=(
            P(("dp", "tensor"), None),
            P(("dp", "tensor"), None),
            P("dp"),
            P("dp", "tensor"),
            P("dp", "tensor"),
            P("dp", "tensor"),
            P("dp", "tensor"),
            P("dp", "tensor"),
            P("dp", "tensor"),
            P("dp", "tensor"),
            P("dp", "tensor", None),
            P("dp", "tensor", None),
            P("dp", "tensor", None),
            P("tensor"),
            P("tensor"),
            P("dp", "tensor"),
            P("dp"),
            P("dp", "tensor"),
            P("dp", "tensor"),
            P("dp", "tensor"),
        ),
        check_vma=False,
    )
```

```python
import jax
import jax.numpy as jnp
from jax import lax
from jax.experimental import pallas as pl
from jax.experimental.pallas import tpu as pltpu
from jax.sharding import PartitionSpec as P

epsilon = 1e-06
CHUNK = 128
LANES = 128
contract_rows = (((0,), (0,)), ((), ()))
contract_cols = (((1,), (1,)), ((), ()))
contract_plain = (((1,), (0,)), ((), ()))
highest = lax.Precision.HIGHEST


def norm_forward(row_values):
    row_scale = lax.rsqrt(jnp.mean(row_values * row_values, axis=-1, keepdims=True) + epsilon)
    return (row_scale, row_values * row_scale)


def norm_backward(grad_normed, unit_values, row_scale, gain_values):
    grad_unit = grad_normed * gain_values
    return row_scale * (
        grad_unit - unit_values * jnp.mean(grad_unit * unit_values, axis=-1, keepdims=True)
    )


def weight_grad(left_in, right_in):
    return lax.dot_general(left_in, right_in, contract_rows, preferred_element_type=jnp.float32)


def times_transpose(left_in, right_in):
    return lax.dot_general(left_in, right_in, contract_cols, preferred_element_type=jnp.float32)


def fine_dot(left_in, right_in, dims=contract_plain):
    return lax.dot_general(
        left_in, right_in, dims, precision=lax.Precision.HIGH, preferred_element_type=jnp.float32
    )


def exact_dot(left_in, right_in, dims=contract_plain):
    return fine_dot(left_in, right_in, dims)


def silu(values):
    return values * lax.logistic(values)


def unit_length(values):
    return values * lax.rsqrt(jnp.sum(values * values, axis=-1, keepdims=True) + epsilon)


def triangle_masks(size):
    row = lax.broadcasted_iota(jnp.int32, (size, size), 0)
    col = lax.broadcasted_iota(jnp.int32, (size, size), 1)
    return row, col


def unit_lower_inverses(lowers):
    size = lowers[0].shape[0]
    row, col = triangle_masks(size)
    eye = jnp.where(row == col, 1.0, 0.0)
    inverses = [eye for _ in lowers]
    bit = 0
    while (1 << bit) < size:
        joined = ((row >> (bit + 1)) == (col >> (bit + 1))) & ((row >> bit) != (col >> bit))
        parts = [jnp.where(joined, lower, 0.0) for lower in lowers]
        if bit == 0:
            inverses = [eye - part for part in parts]
        else:
            inner = [fine_dot(part, inverse) for part, inverse in zip(parts, inverses)]
            steps = [fine_dot(inverse, step) for inverse, step in zip(inverses, inner)]
            inverses = [inverse - step for inverse, step in zip(inverses, steps)]
        bit += 1
    return inverses


@jax.custom_vjp
def known_inverse(lower, inverse):
    return inverse


def known_inverse_fwd(lower, inverse):
    return inverse, inverse


def known_inverse_bwd(inverse, grad):
    turned = inverse.T
    return -fine_dot(fine_dot(turned, grad), turned), jnp.zeros_like(inverse)


known_inverse.defvjp(known_inverse_fwd, known_inverse_bwd)


def each(call, *lists):
    return [call(*items) for items in zip(*lists)]


def mixer_chunk(conv_q, conv_k, conv_v, proj_gate, beta, gate, gain, state, inverter):
    size, key_dim = conv_q[0].shape
    row, col = triangle_masks(size)
    strict = row > col
    lower = row >= col
    query = each(lambda v: unit_length(silu(v)) * key_dim ** (-0.5), conv_q)
    key = each(lambda v: unit_length(silu(v)), conv_k)
    value = each(silu, conv_v)
    wide = each(lambda g: jnp.broadcast_to(g, (size, size)), gate)
    decay_col = each(
        lambda w: jnp.sum(jnp.where(lower, w.T, 0.0), axis=1, keepdims=True), wide
    )
    decay_row = each(
        lambda w: jnp.sum(jnp.where(row <= col, w, 0.0), axis=0, keepdims=True), wide
    )
    decay_end = each(lambda g: jnp.sum(g, axis=0, keepdims=True), gate)
    differ = each(lambda c, r: jnp.where(strict, c - r, 0.0), decay_col, decay_row)
    decay = each(lambda d: jnp.where(lower, jnp.exp(d), 0.0), differ)
    grams = each(lambda k: exact_dot(k, k, contract_cols), key)
    system = each(lambda g, d, b: jnp.where(strict, g * d * b, 0.0), grams, decay, beta)
    inverse = inverter(system)
    grown = each(jnp.exp, decay_col)
    kept = each(lambda k, b, g, s: exact_dot(k * (b * g), s), key, beta, grown, state)
    fresh = each(lambda i, v, b, k: exact_dot(i, v * b - k), inverse, value, beta, kept)
    scores = each(lambda q, k, d: exact_dot(q, k, contract_cols) * d, query, key, decay)
    carried = each(lambda q, g, s: exact_dot(q * g, s), query, grown, state)
    mixed = each(lambda c, s, f: c + exact_dot(s, f), carried, scores, fresh)
    added = each(
        lambda k, e, c, f: exact_dot(k * jnp.exp(e - c), f, contract_rows),
        key, decay_end, decay_col, fresh,
    )
    new_state = each(lambda e, s, a: jnp.exp(e) * s + a, decay_end, state, added)
    gated = each(
        lambda m, g, p: m
        * lax.rsqrt(jnp.mean(m * m, axis=-1, keepdims=True) + epsilon)
        * g
        * silu(p),
        mixed, gain, proj_gate,
    )
    return gated, new_state, inverse


def head_slices(head, heads, key_dim, value_dim):
    q_at = head * key_dim
    k_at = (heads + head) * key_dim
    v_at = 2 * heads * key_dim + head * value_dim
    return (
        slice(q_at, q_at + key_dim),
        slice(k_at, k_at + key_dim),
        slice(v_at, v_at + value_dim),
        slice(head * value_dim, (head + 1) * value_dim),
    )


def head_inputs(heads, key_dim, value_dim, conv_ref, pgate_ref, rates_ref, gain_ref):
    at = [head_slices(head, heads, key_dim, value_dim) for head in range(heads)]
    return at, (
        [conv_ref[:, spots[0]] for spots in at],
        [conv_ref[:, spots[1]] for spots in at],
        [conv_ref[:, spots[2]] for spots in at],
        [pgate_ref[:, spots[3]] for spots in at],
        [rates_ref[:, head : head + 1] for head in range(heads)],
        [rates_ref[:, heads + head : heads + head + 1] for head in range(heads)],
        [gain_ref[:, spots[3]] for spots in at],
    )


def mixer_forward_kernel(
    heads, key_dim, value_dim, conv_ref, pgate_ref, rates_ref, gain_ref,
    gated_ref, states_ref, inverses_ref, state_ref,
):
    @pl.when(pl.program_id(0) == 0)
    def _():
        state_ref[...] = jnp.zeros_like(state_ref)

    at, operands = head_inputs(
        heads, key_dim, value_dim, conv_ref, pgate_ref, rates_ref, gain_ref
    )
    state = [state_ref[head] for head in range(heads)]
    gated, new_state, inverse = mixer_chunk(*operands, state, unit_lower_inverses)
    for head in range(heads):
        gated_ref[:, at[head][3]] = gated[head].astype(gated_ref.dtype)
        states_ref[0, head] = state[head]
        inverses_ref[0, head] = inverse[head]
        state_ref[head] = new_state[head]


def mixer_backward_kernel(
    heads, key_dim, value_dim, conv_ref, pgate_ref, rates_ref, gain_ref, states_ref,
    inverses_ref, grad_ref, gconv_ref, gpgate_ref, grates_ref, ggain_ref, gstate_ref,
):
    @pl.when(pl.program_id(0) == 0)
    def _():
        gstate_ref[...] = jnp.zeros_like(gstate_ref)
        ggain_ref[...] = jnp.zeros_like(ggain_ref)

    lane = lax.broadcasted_iota(jnp.int32, grates_ref.shape, 1)
    rates_grad = jnp.zeros(grates_ref.shape, jnp.float32)
    at, operands = head_inputs(
        heads, key_dim, value_dim, conv_ref, pgate_ref, rates_ref, gain_ref
    )
    inverses = [inverses_ref[0, head] for head in range(heads)]

    def run(*operands):
        gated, new_state, _ = mixer_chunk(
            *operands, lambda systems: each(known_inverse, systems, inverses)
        )
        return gated, new_state

    _, pull = jax.vjp(run, *operands, [states_ref[0, head] for head in range(heads)])
    pulled = pull(
        (
            [grad_ref[:, spots[3]] for spots in at],
            [gstate_ref[head] for head in range(heads)],
        )
    )
    for head in range(heads):
        at_q, at_k, at_v, at_g = at[head]
        gconv_ref[:, at_q] = pulled[0][head]
        gconv_ref[:, at_k] = pulled[1][head]
        gconv_ref[:, at_v] = pulled[2][head]
        gpgate_ref[:, at_g] = pulled[3][head]
        rates_grad = jnp.where(lane == head, pulled[4][head], rates_grad)
        rates_grad = jnp.where(lane == heads + head, pulled[5][head], rates_grad)
        ggain_ref[:, at_g] += pulled[6][head]
        gstate_ref[head] = pulled[7][head]
    grates_ref[...] = rates_grad


def row_block(width, order):
    return pl.BlockSpec((CHUNK, width), lambda step: (order(step), 0))


def mixer_forward(conv_all, proj_gate, rates, gain_row, heads, key_dim, value_dim):
    rows, conv_width = conv_all.shape
    steps = rows // CHUNK
    forward = lambda step: step
    width = heads * value_dim
    return pl.pallas_call(
        lambda *refs: mixer_forward_kernel(heads, key_dim, value_dim, *refs),
        name="mixer_forward",
        grid=(steps,),
        in_specs=[
            row_block(conv_width, forward),
            row_block(width, forward),
            row_block(rates.shape[1], forward),
            pl.BlockSpec((1, width), lambda step: (0, 0)),
        ],
        out_specs=[
            row_block(width, forward),
            pl.BlockSpec((1, heads, key_dim, value_dim), lambda step: (step, 0, 0, 0)),
            pl.BlockSpec((1, heads, CHUNK, CHUNK), lambda step: (step, 0, 0, 0)),
        ],
        out_shape=[
            jax.ShapeDtypeStruct((rows, width), jnp.bfloat16),
            jax.ShapeDtypeStruct((steps, heads, key_dim, value_dim), jnp.float32),
            jax.ShapeDtypeStruct((steps, heads, CHUNK, CHUNK), jnp.float32),
        ],
        scratch_shapes=[pltpu.VMEM((heads, key_dim, value_dim), jnp.float32)],
        cost_estimate=pl.CostEstimate(
            flops=30_000_000_000, bytes_accessed=8_000_000, transcendentals=1_000_000
        ),
    )(conv_all, proj_gate, rates, gain_row)


def mixer_backward(
    conv_all, proj_gate, rates, gain_row, states, inverses, grad_gated, heads, key_dim, value_dim
):
    rows, conv_width = conv_all.shape
    steps = rows // CHUNK
    back = lambda step: steps - 1 - step
    width = heads * value_dim
    return pl.pallas_call(
        lambda *refs: mixer_backward_kernel(heads, key_dim, value_dim, *refs),
        name="mixer_backward",
        grid=(steps,),
        in_specs=[
            row_block(conv_width, back),
            row_block(width, back),
            row_block(rates.shape[1], back),
            pl.BlockSpec((1, width), lambda step: (0, 0)),
            pl.BlockSpec((1, heads, key_dim, value_dim), lambda step: (back(step), 0, 0, 0)),
            pl.BlockSpec((1, heads, CHUNK, CHUNK), lambda step: (back(step), 0, 0, 0)),
            row_block(width, back),
        ],
        out_specs=[
            row_block(conv_width, back),
            row_block(width, back),
            row_block(rates.shape[1], back),
            pl.BlockSpec((1, width), lambda step: (0, 0)),
        ],
        out_shape=[
            jax.ShapeDtypeStruct((rows, conv_width), jnp.float32),
            jax.ShapeDtypeStruct((rows, width), jnp.float32),
            jax.ShapeDtypeStruct(rates.shape, jnp.float32),
            jax.ShapeDtypeStruct((1, width), jnp.float32),
        ],
        scratch_shapes=[pltpu.VMEM((heads, key_dim, value_dim), jnp.float32)],
        cost_estimate=pl.CostEstimate(
            flops=30_000_000_000, bytes_accessed=12_000_000, transcendentals=2_000_000
        ),
    )(conv_all, proj_gate, rates, gain_row, states, inverses, grad_gated)


def ring_position(index, size):
    if size % 2:
        return index
    side, line = index % 2, index // 2
    return line + side * (size - 1 - 2 * line)


def ring_index(position, size):
    if size % 2:
        return position
    side = position // (size // 2)
    line = position + side * (size - 1 - 2 * position)
    return line * 2 + side


def greet(peers):
    barrier = pltpu.get_barrier_semaphore()
    for target in peers:
        pl.semaphore_signal(
            barrier, inc=1, device_id=target, device_id_type=pl.DeviceIdType.MESH
        )
    pl.semaphore_wait(barrier, len(peers))


def send(source, place, sent, landed, target):
    copy = pltpu.make_async_remote_copy(
        src_ref=source,
        dst_ref=place,
        send_sem=sent,
        recv_sem=landed,
        device_id=target,
        device_id_type=pl.DeviceIdType.MESH,
    )
    copy.start()
    return copy


def others(axis):
    ranks = lax.axis_size(axis)
    mine = lax.axis_index(axis)
    return [lax.rem(mine + step, ranks) for step in range(1, ranks)]


def ring_ends(dp):
    at = ring_position(lax.axis_index("dp"), dp)
    after = ring_index((at + 1) % dp, dp)
    before = ring_index((at + dp - 1) % dp, dp)
    return at, after, before


def gather_kernel(dp, ranks, widths, count, *refs):
    parts = len(widths) + 1
    shards, rows = refs[:parts], refs[parts : parts + count]
    full_ref, last_ref, small_ref = refs[parts + count : parts + count + 3]
    gots = refs[parts + count + 3 : parts + 2 * count + 3]
    own_sems, ring_sent, ring_got, row_sent, row_got = refs[parts + 2 * count + 3 :]
    me, mine = lax.axis_index("dp"), lax.axis_index("tensor")
    at, after, before = ring_ends(dp)
    peers = others("tensor")
    ends = [{"dp": after}, {"dp": before}]
    greet(ends + [{"tensor": peer} for peer in peers])
    lefts = [sum(widths[:part]) for part in range(parts)]
    hops = [[(dp - 1 + (part + way) % 2) // 2 for part in range(parts)] for way in range(2)]

    def place(owner, part):
        if part == parts - 1:
            return small_ref.at[owner]
        if part == parts - 2:
            return last_ref.at[owner]
        return full_ref.at[owner, :, pl.ds(lefts[part], widths[part])]

    flying = {}

    def hop(way, step, part):
        owner = ring_index((at + (dp - step if way == 0 else step)) % dp, dp)
        spot = place(owner, part)
        flying[way, step, part] = send(
            shards[part] if step == 0 else spot,
            spot,
            ring_sent.at[way, step, part],
            ring_got.at[way, step, part],
            ends[way],
        )

    for part in range(parts):
        for way in range(2):
            if hops[way][part] > 0:
                hop(way, 0, part)
    swaps = []
    for step, peer in enumerate(peers):
        for index in range(count):
            swaps.append(
                send(
                    rows[index],
                    gots[index].at[mine],
                    row_sent.at[step, index],
                    row_got.at[step, index],
                    {"tensor": peer},
                )
            )
    local = []
    for part in range(parts):
        local.append(pltpu.make_async_copy(shards[part], place(me, part), own_sems.at[part]))
    for index in range(count):
        local.append(
            pltpu.make_async_copy(rows[index], gots[index].at[mine], own_sems.at[parts + index])
        )
    for copy in local:
        copy.start()
    for step in range(1, max(max(line) for line in hops) + 1):
        for part in range(parts):
            for way in range(2):
                if hops[way][part] >= step:
                    flying[way, step - 1, part].wait_recv()
                    if hops[way][part] > step:
                        hop(way, step, part)
    for copy in local + swaps:
        copy.wait()
    for copy in flying.values():
        copy.wait_send()


def gather_all(shards, small, rows, number):
    dp, ranks = lax.axis_size("dp"), lax.axis_size("tensor")
    widths = [shard.shape[1] for shard in shards]
    parts, count = len(shards) + 1, len(rows)
    anywhere = pl.BlockSpec(memory_space=pl.ANY)
    vmem = pl.BlockSpec(memory_space=pltpu.VMEM)
    sem = pltpu.SemaphoreType.DMA
    got = pl.pallas_call(
        lambda *refs: gather_kernel(dp, ranks, widths, count, *refs),
        name="gather_all",
        in_specs=[anywhere] * (parts + count),
        out_specs=[vmem] * (3 + count),
        out_shape=[
            jax.ShapeDtypeStruct((dp, shards[0].shape[0], sum(widths[:-1])), shards[0].dtype),
            jax.ShapeDtypeStruct((dp,) + shards[-1].shape, shards[-1].dtype),
            jax.ShapeDtypeStruct((dp,) + small.shape, small.dtype),
        ]
        + [jax.ShapeDtypeStruct((ranks,) + block.shape, block.dtype) for block in rows],
        scratch_shapes=[
            sem((parts + count,)),
            sem((2, max(1, dp // 2), parts)),
            sem((2, max(1, dp // 2), parts)),
            sem((ranks - 1, count)),
            sem((ranks - 1, count)),
        ],
        compiler_params=pltpu.CompilerParams(collective_id=number, has_side_effects=True),
        cost_estimate=pl.CostEstimate(
            flops=30_000_000_000, bytes_accessed=16_000_000, transcendentals=0
        ),
    )(*shards, small, *rows)
    full, last, *blocks = [block.reshape(-1, block.shape[-1]) for block in got[:2] + got[3:]]
    return full, last, got[2], blocks


def reduce_kernel(dp, ranks, lines, count, cuts, *refs):
    arrays = count[0]
    grads, swaps_in, tile_ref = refs[:arrays], refs[arrays : arrays + count[1]], refs[arrays + count[1]]
    refs = refs[arrays + count[1] + 1 :]
    sums = []
    for cut in cuts:
        sums.append(refs[: len(cut)])
        refs = refs[len(cut) :]
    swaps_out = refs[: count[1]]
    tiles_ref, lines_ref = refs[count[1] : count[1] + 2]
    refs = refs[count[1] + 2 :]
    landed, totals = refs[:arrays], refs[arrays : 2 * arrays]
    ring_sent, ring_got, row_sent, row_got, tile_sent, tile_got, line_sent, line_got = refs[
        2 * arrays :
    ]
    me, mine = lax.axis_index("dp"), lax.axis_index("tensor")
    at, after, before = ring_ends(dp)
    peers, mates = others("tensor"), others("dp")
    ends = [{"dp": after}, {"dp": before}]
    greet([{"dp": mate} for mate in mates] + [{"tensor": peer} for peer in peers])
    last = dp - 2

    def owner(way, step):
        return ring_index((at + (2 * dp - 1 - step if way == 0 else 1 + step)) % dp, dp)

    flying = {}

    def hop(line, step):
        array, top, rows, way = lines[line]
        span = pl.ds(top, rows)
        source = grads[array].at[owner(way, 0), span] if step == 0 else totals[array].at[step - 1, span]
        flying[line, step] = send(
            source,
            landed[array].at[step, span],
            ring_sent.at[line, step],
            ring_got.at[line, step],
            ends[way],
        )

    for line in range(len(lines)):
        hop(line, 0)
    copies = []
    for step, mate in enumerate(mates):
        copies.append(
            send(tile_ref, tiles_ref.at[me], tile_sent.at[step], tile_got.at[step], {"dp": mate})
        )
    for index in range(count[1]):
        for step, peer in enumerate(peers):
            copies.append(
                send(
                    swaps_in[index].at[peer],
                    swaps_out[index].at[mine],
                    row_sent.at[step, index],
                    row_got.at[step, index],
                    {"tensor": peer},
                )
            )
    tiles_ref[me] = tile_ref[...]
    for index in range(count[1]):
        swaps_out[index][mine] = swaps_in[index][mine]
    for step in range(dp - 1):
        for line, (array, top, rows, way) in enumerate(lines):
            flying[line, step].wait_recv()
            span = pl.ds(top, rows)
            own = me if step == last else owner(way, step + 1)
            total = landed[array][step, span].astype(jnp.float32) + grads[array][
                own, span
            ].astype(jnp.float32)
            if step == last:
                for (left, width), sum_ref in zip(cuts[array], sums[array]):
                    sum_ref[span] = total[:, left : left + width]
            else:
                totals[array][step, span] = total.astype(totals[array].dtype)
                hop(line, step + 1)
    small = sums[arrays - 1][0]
    for step, peer in enumerate(peers):
        copies.append(
            send(small, lines_ref.at[mine], line_sent.at[step], line_got.at[step], {"tensor": peer})
        )
    lines_ref[mine] = small[...]
    for copy in copies:
        copy.wait()
    for copy in flying.values():
        copy.wait_send()


def reduce_all(grads, swaps, tile, number, splits):
    dp, ranks = lax.axis_size("dp"), lax.axis_size("tensor")
    vmem = pl.BlockSpec(memory_space=pltpu.VMEM)
    sem = pltpu.SemaphoreType.DMA
    lines = []
    for array, grad in enumerate(grads):
        rows = grad.shape[1]
        pieces = 4 if rows * grad.shape[2] > 100_000 and rows % 64 == 0 else 2
        for piece in range(pieces):
            lines.append((array, piece * rows // pieces, rows // pieces, piece % 2))
    lines = lines[-2:] + lines[:-2]
    count = (len(grads), len(swaps))
    cuts = []
    for widths in splits:
        cuts.append([(sum(widths[:index]), width) for index, width in enumerate(widths)])
    pieces = [
        jax.ShapeDtypeStruct((grad.shape[1], width), jnp.float32)
        for grad, widths in zip(grads, splits)
        for width in widths
    ]
    inputs = list(grads) + list(swaps) + [tile]
    small = grads[-1].shape[1:]
    results = pl.pallas_call(
        lambda *refs: reduce_kernel(dp, ranks, lines, count, cuts, *refs),
        name="reduce_all",
        in_specs=[vmem] * len(inputs),
        out_specs=[vmem] * (len(pieces) + len(swaps) + 2),
        out_shape=pieces
        + [jax.ShapeDtypeStruct(block.shape, block.dtype) for block in swaps]
        + [
            jax.ShapeDtypeStruct((dp,) + tile.shape, tile.dtype),
            jax.ShapeDtypeStruct((ranks,) + small, jnp.float32),
        ],
        scratch_shapes=[pltpu.VMEM((dp - 1,) + grad.shape[1:], grad.dtype) for grad in grads]
        + [pltpu.VMEM((dp - 1,) + grad.shape[1:], grad.dtype) for grad in grads]
        + [
            sem((len(lines), dp - 1)),
            sem((len(lines), dp - 1)),
            sem((ranks - 1, len(swaps))),
            sem((ranks - 1, len(swaps))),
            sem((dp - 1,)),
            sem((dp - 1,)),
            sem((ranks - 1,)),
            sem((ranks - 1,)),
        ],
        compiler_params=pltpu.CompilerParams(collective_id=number, has_side_effects=True),
        cost_estimate=pl.CostEstimate(
            flops=30_000_000_000, bytes_accessed=16_000_000, transcendentals=0
        ),
    )(*inputs)
    arrays = len(pieces)
    return results[:arrays], results[arrays : arrays + len(swaps)], results[-2], results[-1]


def forward_finish(summed, tokens_ref, gain_ref, middle_ref, span):
    middle = tokens_ref[span].astype(jnp.float32) + summed
    middle_ref[span] = middle
    _, unit = norm_forward(middle)
    return unit * gain_ref[...]


def backward_finish(summed, cotangent_ref, gain_ref, middle_ref, grad_ref, gain_grad_ref, span):
    scale, unit = norm_forward(middle_ref[span])
    gain_grad_ref[...] += jnp.sum(summed * unit, axis=0, keepdims=True)
    grad = cotangent_ref[span].astype(jnp.float32) + norm_backward(
        summed, unit, scale, gain_ref[...]
    )
    grad_ref[span] = grad
    return grad


def turn_kernel(ranks, chunks, backward, *refs):
    if backward:
        part_ref, rows_ref, gain_ref, middle_ref, got_ref, grad_ref, gain_grad_ref = refs[:7]
        scratch = refs[7:]
        gain_grad_ref[...] = jnp.zeros_like(gain_grad_ref)
    else:
        part_ref, rows_ref, gain_ref, got_ref, middle_ref = refs[:5]
        scratch = refs[5:]
    pair_buf, sum_buf, far_buf, pair_s, pair_r, far_s, far_r, out_s, out_r, on_s, on_r = scratch
    mine = lax.axis_index("tensor")
    side, group = mine % 2, mine // 2
    groups = ranks // 2
    partner = group * 2 + 1 - side
    away = [(group + step) % groups for step in range(1, groups)]
    mates = [{"tensor": other * 2 + side} for other in away]
    near = {"tensor": partner}
    greet([near] + mates)
    rows = part_ref.shape[1] // chunks
    flying = []
    spans = [pl.ds(chunk * rows, rows) for chunk in range(chunks)]

    def go(*operands):
        copy = send(*operands)
        flying.append(copy)
        return copy

    pairs, fars, outs, ons, backs = {}, {}, {}, {}, {}
    order = away + [group]
    for chunk, span in enumerate(spans):
        for step, other in enumerate(order):
            pairs[step, chunk] = go(
                part_ref.at[other * 2 + 1 - side, span],
                pair_buf.at[step, span],
                pair_s.at[step, chunk],
                pair_r.at[step, chunk],
                near,
            )
    for chunk, span in enumerate(spans):
        for step, other in enumerate(away):
            pairs[step, chunk].wait_recv()
            total = part_ref[other * 2 + side, span].astype(jnp.float32) + pair_buf[
                step, span
            ].astype(jnp.float32)
            sum_buf[step, span] = total.astype(sum_buf.dtype)
            fars[step, chunk] = go(
                sum_buf.at[step, span],
                far_buf.at[step, span],
                far_s.at[step, chunk],
                far_r.at[step, chunk],
                mates[step],
            )
    for chunk, span in enumerate(spans):
        pairs[groups - 1, chunk].wait_recv()
        summed = part_ref[mine, span].astype(jnp.float32) + pair_buf[groups - 1, span].astype(
            jnp.float32
        )
        for step in range(groups - 1):
            fars[step, chunk].wait_recv()
            summed = summed + far_buf[step, span].astype(jnp.float32)
        if backward:
            done = backward_finish(
                summed, rows_ref, gain_ref, middle_ref, grad_ref, gain_grad_ref, span
            )
        else:
            done = forward_finish(summed, rows_ref, gain_ref, middle_ref, span)
        got_ref[mine, span] = done.astype(got_ref.dtype)
        place = got_ref.at[mine, span]
        for step in range(groups - 1):
            outs[step, chunk] = go(
                place, place, out_s.at[step, chunk], out_r.at[step, chunk], mates[step]
            )
        ons[groups - 1, chunk] = go(
            place, place, on_s.at[groups - 1, chunk], on_r.at[groups - 1, chunk], near
        )
    for chunk, span in enumerate(spans):
        for step in range(groups - 1):
            outs[step, chunk].wait_recv()
            source = ((group + groups - 1 - step) % groups) * 2 + side
            place = got_ref.at[source, span]
            ons[step, chunk] = go(
                place, place, on_s.at[step, chunk], on_r.at[step, chunk], near
            )
    for chunk in range(chunks):
        for step in range(groups):
            ons[step, chunk].wait_recv()
    for copy in flying:
        copy.wait_send()


def turn(part, own_rows, gain, number, middle=None, chunks=4):
    ranks = lax.axis_size("tensor")
    rows, model = own_rows.shape
    chunks = chunks if rows % (16 * chunks) == 0 else 1
    groups = ranks // 2
    backward = middle is not None
    vmem = pl.BlockSpec(memory_space=pltpu.VMEM)
    sem = pltpu.SemaphoreType.DMA
    out_shape = [
        jax.ShapeDtypeStruct((ranks, rows, model), jnp.bfloat16),
        jax.ShapeDtypeStruct((rows, model), jnp.float32),
    ]
    inputs = [part.reshape(ranks, rows, model), own_rows, gain]
    if backward:
        out_shape.append(jax.ShapeDtypeStruct((1, model), jnp.float32))
        inputs.append(middle)
    results = pl.pallas_call(
        lambda *refs: turn_kernel(ranks, chunks, backward, *refs),
        name="turn_backward" if backward else "turn_forward",
        in_specs=[vmem] * len(inputs),
        out_specs=[vmem] * len(out_shape),
        out_shape=out_shape,
        scratch_shapes=[
            pltpu.VMEM((groups, rows, model), jnp.bfloat16),
            pltpu.VMEM((max(1, groups - 1), rows, model), jnp.bfloat16),
            pltpu.VMEM((max(1, groups - 1), rows, model), jnp.bfloat16),
        ]
        + [sem((groups, chunks))] * 8,
        compiler_params=pltpu.CompilerParams(collective_id=number, has_side_effects=True),
        cost_estimate=pl.CostEstimate(
            flops=10_000_000_000, bytes_accessed=4_000_000, transcendentals=0
        ),
    )(*inputs)
    return (results[0].reshape(-1, model),) + tuple(results[1:])


def short_conv(inputs, weights):
    tap_count = weights.shape[0]
    row_count = inputs.shape[0]
    padded = jnp.pad(inputs, ((tap_count - 1, 0), (0, 0)))
    result = jnp.zeros_like(inputs)
    for offset in range(tap_count):
        result = result + padded[offset : offset + row_count] * weights[offset]
    return result


def round_up(size, step):
    return -(-size // step) * step


def pad_columns(matrix_in, width):
    return jnp.pad(matrix_in, ((0, 0), (0, width - matrix_in.shape[1])))


def tap_rows(conv_weights):
    channels, heads, taps = conv_weights.shape
    return jnp.transpose(conv_weights, (1, 2, 0)).reshape(heads * taps, channels)


def joined_taps(rows, heads):
    shards, _, channels = rows.shape
    split = rows.reshape(shards, heads, -1, channels)
    taps = split.shape[2]
    return jnp.transpose(split, (2, 1, 0, 3)).reshape(taps, heads * shards * channels)


def split_taps(taps_in, heads, shards):
    taps, width = taps_in.shape
    split = taps_in.reshape(taps, heads, shards, width // (heads * shards))
    return jnp.transpose(split, (2, 1, 0, 3)).reshape(shards, heads * taps, -1)


def rate_terms(proj_beta, proj_alpha, log_rate, rate_bias):
    log_gates = -jnp.exp(log_rate) * jax.nn.softplus(proj_alpha + rate_bias)
    return jnp.concatenate([jax.nn.sigmoid(proj_beta), log_gates], axis=1)


def on_device(
    tokens, cotangent, norm1_gain, w_query, w_key, w_value, w_gate_out, w_out, w_beta, w_alpha,
    conv_query, conv_key, conv_value, a_log, dt_bias, head_gain, norm2_gain, w_up_gate, w_up,
    w_down,
):
    bf16, f32 = jnp.bfloat16, jnp.float32
    shard_rows, model = w_query.shape[0], tokens.shape[1]
    dp = model // shard_rows
    heads = a_log.shape[0]
    key_dim, value_dim = w_query.shape[1] // heads, w_value.shape[1] // heads
    taps = conv_query.shape[2]
    tap_lines = heads * taps
    qk_width, v_width = heads * key_dim, heads * value_dim
    conv_width = 2 * qk_width + v_width
    in_width = conv_width + v_width
    hidden_width = w_up.shape[1]
    ff = round_up(hidden_width, 256)

    packed = [tap_rows(conv_query), tap_rows(conv_key), tap_rows(conv_value), head_gain.T]
    lanes = [block.shape[1] for block in packed]
    lefts = [sum(lanes[:index]) for index in range(4)]
    line_rows = tap_lines + 2 + 2 * heads
    small_rows = round_up(line_rows, 16)
    small_width = round_up(max(sum(lanes), shard_rows), LANES)

    def small_block(groups, lines, kind):
        shards = groups[0].shape[0]
        group = jnp.concatenate(
            [jnp.pad(g, ((0, 0), (0, tap_lines - g.shape[1]), (0, 0))) for g in groups], axis=2
        )
        group = jnp.pad(group, ((0, 0), (0, 0), (0, small_width - sum(lanes))))
        lines = jnp.pad(lines, ((0, 0), (0, 0), (0, small_width - lines.shape[2])))
        rest = jnp.zeros((shards, small_rows - line_rows, small_width), kind)
        return jnp.concatenate([group.astype(kind), lines.astype(kind), rest], axis=1)

    small = small_block(
        [block[None] for block in packed],
        jnp.concatenate([norm1_gain[None], norm2_gain[None], w_beta.T, w_alpha.T], axis=0)[None],
        bf16,
    )[0]
    ffn_pack = jnp.concatenate([pad_columns(w, ff) for w in (w_up_gate, w_up, w_down)], axis=1)
    qk_full, value_full, small_full, (tokens_got,) = gather_all(
        [w_query, w_key, w_value], small, [tokens], 1
    )
    small_full, ffn_pack, gate_in = lax.optimization_barrier((small_full, ffn_pack, w_gate_out))
    ffn_full = lax.all_gather(ffn_pack, "dp", axis=0, tiled=True)
    gate_full, out_full, _, (cot_full,) = gather_all([gate_in, w_out], small, [cotangent], 2)
    small_all = small_full.astype(f32)

    def group_of(index, rows):
        return small_all[:, :rows, lefts[index] : lefts[index] + lanes[index]]

    def line_of(first, count):
        lines = small_all[:, tap_lines + first : tap_lines + first + count, :shard_rows]
        return jnp.swapaxes(lines, 0, 1).reshape(count, model)

    gain_one, gain_two = line_of(0, 1), line_of(1, 1)
    rate_weights = line_of(2, 2 * heads).astype(bf16)
    conv_weights = jnp.concatenate(
        [joined_taps(group_of(index, tap_lines), heads) for index in range(3)], axis=1
    )
    gain_row = joined_taps(group_of(3, heads), heads)

    tokens_full = tokens_got.astype(f32)
    _, unit_full = norm_forward(tokens_full)
    normed_one = (unit_full * gain_one).astype(bf16)
    in_parts = (qk_full, value_full, gate_full)
    in_edges = (0, 2 * qk_width, conv_width, in_width)
    proj_qk, proj_value, proj_gate = [
        jnp.dot(normed_one, part, preferred_element_type=f32) for part in in_parts
    ]
    proj_rates = times_transpose(normed_one, rate_weights)
    proj_conv = jnp.concatenate([proj_qk, proj_value], axis=1)
    conv_all, conv_pull = jax.vjp(short_conv, proj_conv, conv_weights)
    rates, rates_pull = jax.vjp(
        rate_terms, proj_rates[:, :heads], proj_rates[:, heads:], a_log.astype(f32),
        dt_bias.astype(f32),
    )
    mixed, states, inverses = mixer_forward(
        conv_all, proj_gate, rates, gain_row, heads, key_dim, value_dim
    )
    row_values = tokens.astype(f32)
    scale_one, unit_one = norm_forward(row_values)
    normed_two, middle = turn(
        times_transpose(mixed, out_full).astype(bf16), tokens, gain_two, 4
    )
    gates_full, down_full = ffn_full[:, : 2 * ff], ffn_full[:, 2 * ff :]
    grad_hidden = jnp.dot(cot_full, down_full, preferred_element_type=f32)
    ups = jnp.dot(normed_two, gates_full, preferred_element_type=f32)
    up_gate, up_lin = ups[:, :ff], ups[:, ff:]
    gate_sigmoid = jax.nn.sigmoid(up_gate)
    hidden = (up_gate * gate_sigmoid * up_lin).astype(bf16)
    grad_gate = (
        grad_hidden * up_lin * gate_sigmoid * (1.0 + up_gate * (1.0 - gate_sigmoid))
    ).astype(bf16)
    grad_lin = (grad_hidden * up_gate * gate_sigmoid).astype(bf16)
    grad_ups = jnp.concatenate([grad_gate, grad_lin], axis=1)
    ffn_grads = jnp.concatenate(
        [
            weight_grad(normed_two, grad_ups).astype(bf16),
            weight_grad(cot_full, hidden).astype(bf16),
        ],
        axis=1,
    )
    grad_normed_part_two = times_transpose(grad_ups, gates_full).astype(bf16)
    grad_normed_part_two, ffn_grads = lax.optimization_barrier((grad_normed_part_two, ffn_grads))
    ffn_sums = lax.psum_scatter(ffn_grads, "dp", scatter_dimension=0, tiled=True)
    mid_full, grad_middle, grad_gain_two = turn(
        grad_normed_part_two, cotangent, gain_two, 3, middle
    )
    ranks = lax.axis_size("tensor")
    out_grads = weight_grad(mid_full, mixed).astype(bf16)
    result_part = times_transpose(hidden, down_full).astype(bf16)

    grad_mixed = jnp.dot(mid_full, out_full, preferred_element_type=f32)
    grad_conv_all, grad_pgate, grad_rates, grad_gain_row = mixer_backward(
        conv_all, proj_gate, rates, gain_row, states, inverses, grad_mixed,
        heads, key_dim, value_dim,
    )
    grad_pconv, grad_conv_w = conv_pull(grad_conv_all)
    grad_beta, grad_alpha, grad_rate_part, grad_bias_part = rates_pull(grad_rates)
    grad_proj = jnp.concatenate([grad_pconv.astype(bf16), grad_pgate.astype(bf16)], axis=1)
    grad_rate_proj = jnp.concatenate([grad_beta, grad_alpha], axis=1).astype(bf16)
    grad_normed_part = jnp.dot(grad_rate_proj, rate_weights, preferred_element_type=f32)
    for index, part in enumerate(in_parts):
        left, right = in_edges[index : index + 2]
        grad_normed_part = grad_normed_part + times_transpose(grad_proj[:, left:right], part)
    grad_gain_one = jnp.sum(grad_normed_part * unit_full, axis=0)
    grad_lines = jnp.concatenate(
        [grad_gain_one[None], grad_gain_two, weight_grad(grad_rate_proj, normed_one)], axis=0
    )
    edges = [0, qk_width, 2 * qk_width, conv_width]
    grad_small = small_block(
        [split_taps(grad_conv_w[:, edges[i] : edges[i + 1]], heads, dp) for i in range(3)]
        + [split_taps(grad_gain_row, heads, dp)],
        jnp.swapaxes(grad_lines.reshape(2 + 2 * heads, dp, shard_rows), 0, 1),
        f32,
    )
    rate_line = jnp.concatenate([grad_rate_part, grad_bias_part])
    rate_tile = jnp.pad(rate_line[None], ((0, 7), (0, LANES - 2 * heads)))
    in_grads = weight_grad(normed_one, grad_proj).astype(bf16)
    sums, swapped, rate_tiles, small_lines = reduce_all(
        [
            in_grads.reshape(dp, shard_rows, in_width),
            out_grads.reshape(dp, shard_rows, v_width),
            grad_small,
        ],
        [
            grad_normed_part.astype(bf16).reshape(ranks, -1, model),
            result_part.reshape(ranks, -1, model),
        ],
        rate_tile,
        7,
        [[qk_width, qk_width, v_width, v_width], [v_width], [small_width]],
    )
    query_sums, key_sums, value_sums, gate_sums, out_sums, small_sums = sums
    grad_normed_one = jnp.sum(swapped[0].astype(f32), axis=0)
    result = (middle + jnp.sum(swapped[1].astype(f32), axis=0)).astype(bf16)
    grad_rows = grad_middle + norm_backward(grad_normed_one, unit_one, scale_one, gain_one)
    rate_sums = jnp.sum(rate_tiles, axis=0)[0]
    gain_sums = jnp.sum(small_lines[:, tap_lines : tap_lines + 2, :shard_rows], axis=0)
    ffn_sums = ffn_sums.astype(f32)

    def taps_out(index, lines):
        block = small_sums[:lines, lefts[index] : lefts[index] + lanes[index]]
        return jnp.transpose(block.reshape(heads, -1, lanes[index]), (2, 0, 1))

    def lines_out(first):
        return small_sums[tap_lines + first : tap_lines + first + heads, :shard_rows].T

    return (
        result,
        grad_rows,
        gain_sums[0],
        query_sums,
        key_sums,
        value_sums,
        gate_sums,
        out_sums,
        lines_out(2),
        lines_out(2 + heads),
        taps_out(0, tap_lines),
        taps_out(1, tap_lines),
        taps_out(2, tap_lines),
        rate_sums[:heads],
        rate_sums[heads : 2 * heads],
        taps_out(3, heads)[:, :, 0],
        gain_sums[1],
        ffn_sums[:, :hidden_width],
        ffn_sums[:, ff : ff + hidden_width],
        ffn_sums[:, 2 * ff : 2 * ff + hidden_width],
    )


def solution(mesh):
    placed = (
        P(("dp", "tensor"), None),
        P(("dp", "tensor"), None),
        P("dp"),
        P("dp", "tensor"),
        P("dp", "tensor"),
        P("dp", "tensor"),
        P("dp", "tensor"),
        P("dp", "tensor"),
        P("dp", "tensor"),
        P("dp", "tensor"),
        P("dp", "tensor", None),
        P("dp", "tensor", None),
        P("dp", "tensor", None),
        P("tensor"),
        P("tensor"),
        P("dp", "tensor"),
        P("dp"),
        P("dp", "tensor"),
        P("dp", "tensor"),
        P("dp", "tensor"),
    )
    return jax.shard_map(
        on_device,
        mesh=mesh,
        in_specs=placed,
        out_specs=(
            P(("dp", "tensor"), None),
            P(("dp", "tensor"), None),
            P("dp"),
            P("dp", "tensor"),
            P("dp", "tensor"),
            P("dp", "tensor"),
            P("dp", "tensor"),
            P("dp", "tensor"),
            P("dp", "tensor"),
            P("dp", "tensor"),
            P("dp", "tensor", None),
            P("dp", "tensor", None),
            P("dp", "tensor", None),
            P("tensor"),
            P("tensor"),
            P("dp", "tensor"),
            P("dp"),
            P("dp", "tensor"),
            P("dp", "tensor"),
            P("dp", "tensor"),
        ),
        check_vma=False,
    )
```
